32 devices in a mesh: patch: 2 (over y), exp: 4 (over z), tile: 2 (over x), band: 2 (over core).
Axes of the slice: x: 2, y: 2, z: 4, core: 2. Of those that a mesh axis runs over, the one named last changes fastest.
Arguments:
- images: bfloat16 [4, 2, 64, 128, 128], P(('patch', 'band'), 'tile', 'exp'), parts along dimension 0, may hold values from -6 to 6
- mask_bits: int32 [4, 2, 64, 128, 128], P(('patch', 'band'), 'tile', 'exp'), parts along dimension 0, may hold values from 0 to 7
- inv_var: float32 [4, 2, 64], P(('patch', 'band'), 'tile', 'exp'), parts along dimension 0, may hold values from 0.5 to 4
- routes: int32 [4, 2, 64, 1], P(('patch', 'band'), 'tile', 'exp'), parts along dimension 0, may hold values from 0 to 3; in each aligned block of 16 rows (0 to 15, 16 to 31, ..., all dimensions but the last counted through in order) at most 8 rows name the same one
- block_slot: int32 [4, 2, 64], P(('patch', 'band'), 'tile', 'exp'), parts along dimension 0, may hold values from 0 to 7
- kernel_index: int32 [4, 2, 64], P(('patch', 'band'), 'tile', 'exp'), parts along dimension 0, may hold values from 0 to 63
- coefficients: float32 [64, 3], replicated, may hold values from -4 to 4
Outputs:
- coadd: float32 [4, 512, 2048], P(('patch', 'band'), 'tile', 'exp'), parts along dimension 0
- detection: float32 [1024, 2048], P(('patch', 'tile'), 'exp'), parts along dimension 0
The draws below stay inside these ranges and needn't reach their ends.
There are 2 independent parts, one for each index of `patch`. The reference program is written for one: setup_inputs(seed, part) draws one part's arguments, and reference() takes and returns one part's arrays. A program takes and returns all parts, laid end to end along the dimension named above; an argument that names none is the same for every part. Nothing has to cross between parts.
Inputs may be any that keep to these rules, and one draw needn't show every extreme that they name: Among the 16 sub-blocks of one device for one band and strip (an aligned block of routes), no tile column is named more than 8 times, and some tile column is named exactly 8 times.
All inputs are finite; a program needn't handle non-finite values.
Results may differ from the reference program's by a relative error of at most 0.0039.
Values may be sent and summed in bfloat16 or wider, within the bound.
A program may use at most 128 MiB of HBM per device.

```python
import math
import jax
import jax.numpy as jnp
import numpy as np
from jax import lax

BLOCK = 128
TAPS = 41
NCOEF = 64
SB = 16
BLOCK_ROWS = 2
BLOCK_COLS = 4
CAP = 8
SUBS = 64
STRIPS = 2
BANDS = 2
N_EXP = 4


def touch_ends(values, own_key, low, top_value):
    extent = values.shape
    index_at = [jax.random.randint(jax.random.fold_in(own_key, axis), (), 0, extent[axis]) for axis in range(len(extent))]
    values = values.at[tuple(index_at)].set(low)
    longest = extent.index(max(extent))
    index_at[longest] = (index_at[longest] + 1) % extent[longest]
    return values.at[tuple(index_at)].set(top_value)


def levels(stream_key, shape, shards, least, largest):
    loudness = 1.0
    for dim, blocks in shards:
        draws = jax.random.uniform(jax.random.fold_in(jax.random.fold_in(stream_key, 6), dim), (blocks,), jnp.float32, least / len(shards), largest / len(shards))
        loudness = loudness * jnp.repeat(jnp.exp(draws), shape[dim] // blocks).reshape((-1,) + (1,) * (len(shape) - 1 - dim))
    return loudness


def routed_block(own_key, own, number, rows, amount, top, limit, skew):
    ranking = jax.random.permutation(own_key, amount)
    packed, common = load_shares(amount, rows * top, limit, skew, True), load_shares(amount, rows * top, limit, skew, False)
    places = jnp.arange(amount)

    def named(lengths, offset_by):
        used = int((lengths > 0).sum())
        fixed = max(1, used // 4)
        moved = fixed + (places - fixed + offset_by * (used - fixed)) % max(1, amount - fixed)
        return jnp.zeros((amount,), jnp.int32).at[ranking[jnp.where(places < fixed, places, moved)]].set(jnp.asarray(lengths, jnp.int32))

    lengths = jnp.where(number % 4 == 0, named(packed, number // 4), named(common, number - number // 4 - 1))
    mixed = jax.random.permutation(jax.random.fold_in(own, 3), amount)
    source_of, taker = mixed[0:amount // 2 * 2:2], mixed[1:amount // 2 * 2:2]
    slack = jnp.minimum(lengths[source_of] - 1, limit - lengths[taker]) // 2
    slack = jnp.where((source_of == ranking[0]) | (taker == ranking[0]) | (lengths[taker] == 0), 0, jnp.maximum(slack, 0))
    moved = jax.random.randint(jax.random.fold_in(own, 4), (amount // 2,), 0, 1 << 20) % (slack + 1)
    lengths = lengths.at[source_of].add(-moved).at[taker].add(moved)
    items = jnp.searchsorted(jnp.cumsum(lengths), jnp.arange(rows * top), side="right").astype(jnp.int32)
    table = items.reshape(top, rows).T
    table = table[jax.random.permutation(jax.random.fold_in(own, 1), rows)]
    offset_by = jax.random.randint(jax.random.fold_in(own, 2), (rows, 1), 0, top)
    return jnp.take_along_axis(table, (jnp.arange(top)[None, :] + offset_by) % top, axis=1)


def load_shares(number_of, total, most, skew, full):
    weights = [(1 << 20) // math.isqrt(rank ** skew) + 1 for rank in range(1, number_of + 1)]
    largest = most if full else min(most, max(-(-total // number_of), total * weights[0] // sum(weights)))
    least = 1 if total - largest >= number_of - 1 else 0
    holding, rest = [largest] + [least] * (number_of - 1), total - largest - least * (number_of - 1)
    while rest > 0:
        candidates = [i for i in range(1, number_of) if holding[i] < largest] or [i for i in range(1, number_of) if holding[i] < most]
        pool, left = sum([weights[i] for i in candidates]), rest
        for i in candidates:
            extra = min(most - holding[i], max(1, left * weights[i] // pool), rest)
            holding[i] = holding[i] + extra
            rest = rest - extra
    return np.array(holding)


def noise(key, dims, scale, limit, pieces=(), kind=jnp.bfloat16):
    factor_of = levels(key, dims, pieces, -0.22, 0.18) if pieces else 1.0
    array = jax.random.normal(key, dims, jnp.float32) * scale * factor_of
    return jnp.minimum(jnp.maximum(array, -limit), limit).astype(kind)


def setup_inputs(seed: int = 0, part: int = 0) -> dict:
    arg_keys = jax.random.split(jax.random.key(seed), 8)
    own_keys = jax.random.split(jax.random.fold_in(arg_keys[7], part), 8)
    images = noise(own_keys[0], (BANDS, STRIPS, SUBS, BLOCK, BLOCK), 1.0, 6.0, ((0, 2), (1, 2), (2, 4)))
    mask_bits = touch_ends(jax.random.randint(own_keys[1], (BANDS, STRIPS, SUBS, BLOCK, BLOCK), 0, 8), jax.random.fold_in(own_keys[1], 1), 0, 7).astype(jnp.int32)
    inv_var = jnp.clip(jnp.exp(math.log(4.0) - 2.0794415 * jax.random.uniform(own_keys[2], (BANDS, STRIPS, SUBS), jnp.float32) ** levels(own_keys[2], (BANDS, STRIPS, SUBS), ((0, 2), (1, 2), (2, 4)), -0.2, 0.2)), 0.5, 4.0)
    routes_keys = jax.random.split(jax.random.fold_in(own_keys[3], 1), BANDS * STRIPS * SUBS // SB)
    routes_turns = jax.random.permutation(jax.random.fold_in(own_keys[3], 3), BANDS * STRIPS * SUBS // SB)
    routes = jax.vmap(lambda own, number: routed_block(jax.random.fold_in(own_keys[3], 2), own, number, SB, N_EXP, 1, CAP, 2))(routes_keys, routes_turns).reshape((BANDS, STRIPS, SUBS, 1))
    block_slot = touch_ends(jax.random.randint(own_keys[4], (BANDS, STRIPS, SUBS), 0, BLOCK_ROWS * BLOCK_COLS), jax.random.fold_in(own_keys[4], 1), 0, (BLOCK_ROWS * BLOCK_COLS) - 1).astype(jnp.int32)
    kernel_index = touch_ends(jax.random.randint(own_keys[5], (BANDS, STRIPS, SUBS), 0, NCOEF), jax.random.fold_in(own_keys[5], 1), 0, NCOEF - 1).astype(jnp.int32)
    coefficients = noise(arg_keys[6], (NCOEF, 3), 1.0, 4.0, (), jnp.float32)
    return dict(images=images, mask_bits=mask_bits, inv_var=inv_var, routes=routes, block_slot=block_slot, kernel_index=kernel_index, coefficients=coefficients)


kernel_sigmas = (1.0, 2.5, 6.0)


def usable_share(bits):
    flagged = jnp.bitwise_and(bits, 6) == 6
    suspect = jnp.bitwise_and(bits, 1).astype(jnp.float32)
    return jnp.where(flagged, 0.0, 1.0 - 0.5 * suspect).astype(jnp.float32)


def gaussian_taps(half_span):
    taps_axis = jnp.arange(-half_span, half_span + 1).astype(jnp.float32)
    result = []
    for spread in kernel_sigmas:
        values = jnp.exp(-taps_axis * taps_axis / (2.0 * spread * spread))
        result.append(values / jnp.sum(values))
    return jnp.stack(result)


def to_image(blocks):
    grid_rows, grid_cols = blocks.shape[0], blocks.shape[1]
    return blocks.transpose(0, 2, 1, 3).reshape(grid_rows * BLOCK, grid_cols * BLOCK)


def reference(images, mask_bits, inv_var, routes, block_slot, kernel_index, coefficients):
    half_span = TAPS // 2
    taps = gaussian_taps(half_span)
    grid_rows = STRIPS * BLOCK_ROWS
    grid_cols = N_EXP * BLOCK_COLS
    strip_of = jnp.repeat(jnp.arange(STRIPS, dtype=jnp.int32), SUBS)
    coadds = []
    detection = jnp.zeros((grid_rows * BLOCK, grid_cols * BLOCK), jnp.float32)
    for band_index in range(BANDS):
        usable = usable_share(mask_bits[band_index].reshape(-1, BLOCK, BLOCK))
        inverse = inv_var[band_index].reshape(-1)[:, None, None]
        weight = (usable * inverse).astype(jnp.bfloat16)
        pictures = images[band_index].reshape(-1, BLOCK, BLOCK).astype(jnp.float32)
        weighted = (usable * inverse * pictures).astype(jnp.bfloat16)
        slot_here = block_slot[band_index].reshape(-1).astype(jnp.int32)
        owner = routes[band_index].reshape(-1).astype(jnp.int32)
        block_row = (strip_of * BLOCK_ROWS + slot_here // BLOCK_COLS).astype(jnp.int32)
        block_col = (owner * BLOCK_COLS + slot_here % BLOCK_COLS).astype(jnp.int32)
        coef_rows = coefficients[kernel_index[band_index].reshape(-1).astype(jnp.int32)]
        empty = jnp.zeros((grid_rows, grid_cols, BLOCK, BLOCK), jnp.float32)
        planes = []
        for basis_index in range(3):
            contrib = coef_rows[:, basis_index][:, None, None] * weighted.astype(jnp.float32)
            planes.append(to_image(empty.at[block_row, block_col].add(contrib)))
        depth_sum = to_image(empty.at[block_row, block_col].add(weight.astype(jnp.float32)))
        stacked = jnp.stack(planes)[None]
        downward = lax.conv_general_dilated(stacked, taps[:, None, :, None], (1, 1), ((half_span, half_span), (0, 0)), dimension_numbers=("NCHW", "OIHW", "NCHW"), feature_group_count=3, precision=lax.Precision.HIGHEST)
        sideways = lax.conv_general_dilated(downward, taps[:, None, None, :], (1, 1), ((0, 0), (half_span, half_span)), dimension_numbers=("NCHW", "OIHW", "NCHW"), feature_group_count=3, precision=lax.Precision.HIGHEST)
        matched = jnp.sum(sideways[0], axis=0)
        denominator = 1.0 + depth_sum
        coadded = matched / denominator
        coadds.append(coadded)
        detection = detection + coadded * coadded * denominator
    return jnp.stack(coadds), detection
```

```python
import functools

import jax
import jax.numpy as jnp
import numpy as np
from jax import lax
from jax.experimental import pallas as pl
from jax.experimental.pallas import tpu as pltpu
from jax.sharding import PartitionSpec as P

BLOCK = 128
TAPS = 41
BLOCK_ROWS = 2
BLOCK_COLS = 4
SPILL = 32

kernel_sigmas = (1.0, 2.5, 6.0)
MESH = pl.DeviceIdType.MESH


def tap_matrix(rows, cols, shift):
    half_span = TAPS // 2
    offset = np.arange(rows)[:, None] - np.arange(cols)[None, :] - shift
    axis = np.arange(-half_span, half_span + 1).astype(np.float64)
    result = []
    for spread in kernel_sigmas:
        norm = np.sum(np.exp(-axis * axis / (2.0 * spread * spread)))
        result.append(
            np.where(
                np.abs(offset) <= half_span,
                np.exp(-offset * offset / (2.0 * spread * spread)),
                0.0,
            )
            / norm
        )
    return np.stack(result)


def tap_pair(taps):
    high = taps.astype(jnp.bfloat16)
    low = (taps - high.astype(np.float64)).astype(jnp.bfloat16)
    return jnp.asarray(np.stack([high, low]))


def split(value):
    high = value.astype(jnp.bfloat16)
    return high, (value - high.astype(jnp.float32)).astype(jnp.bfloat16)


def dot3(left, right):
    (left_high, left_low), (right_high, right_low) = left, right
    dot = functools.partial(jnp.dot, preferred_element_type=jnp.float32)
    return dot(left_high, right_high) + (dot(left_high, right_low) + dot(left_low, right_high))


def place_kernel(
    n, held, me, routes, slots, kernels, inverse, coefs, images, masks, across, down,
    depth, matched, own, spill_up, spill_down, acc, wide,
):
    blocks = BLOCK_ROWS * BLOCK_COLS
    tile_rows = BLOCK_ROWS * BLOCK
    tile_cols = BLOCK_COLS * BLOCK
    half = tile_cols // 2
    wide[...] = jnp.zeros_like(wide)

    def place(d, carry):
        acc[...] = jnp.zeros_like(acc)

        def one(i, carry):
            @pl.when(routes[i] == d)
            def _():
                slot = slots[i]
                which = kernels[i]
                row = slot // BLOCK_COLS
                col = slot % BLOCK_COLS
                rows = pl.ds(pl.multiple_of(row * BLOCK, BLOCK), BLOCK)
                cols = pl.ds(pl.multiple_of(col * BLOCK, BLOCK), BLOCK)
                bits = masks[i]
                suspect = jnp.bitwise_and(bits, 1).astype(jnp.float32)
                usable = jnp.where(
                    jnp.bitwise_and(bits, 6) == 6, 0.0, 1.0 - 0.5 * suspect
                )
                scaled = usable * inverse[i]
                weighted = (
                    (scaled * images[i].astype(jnp.float32))
                    .astype(jnp.bfloat16)
                    .astype(jnp.float32)
                )
                weight = scaled.astype(jnp.bfloat16).astype(jnp.float32)
                for k in range(3):
                    acc[k, rows, cols] += coefs[which, k] * weighted
                acc[3, rows, cols] += weight

            return carry

        lax.fori_loop(0, held, one, 0)
        depth[d] = acc[3].astype(jnp.bfloat16)
        highs, lows = [], []
        for k in range(3):
            tall = dot3((down[0, k], down[1, k]), split(acc[k]))
            high, low = split(tall)
            highs.append(high)
            lows.append(low)
        base = d * tile_cols
        for piece in range(3):
            left = max(0, piece - 1) * half
            right = min(2, piece + 1) * half
            top = left - (piece - 1) * half
            total = None
            for k in range(3):
                term = dot3(
                    (highs[k][:, left:right], lows[k][:, left:right]),
                    (
                        across[0, k, top : top + right - left],
                        across[1, k, top : top + right - left],
                    ),
                )
                total = term if total is None else total + term
            start = pl.multiple_of(base + piece * half, BLOCK)
            wide[:, pl.ds(start, half)] += total
        return carry

    lax.fori_loop(0, n, place, 0)

    def emit(d, carry):
        start = pl.multiple_of(BLOCK + d * tile_cols, BLOCK)
        cols = pl.ds(start, tile_cols)
        matched[d] = wide[SPILL : SPILL + tile_rows, cols].astype(jnp.bfloat16)
        spill_up[d] = wide[0:SPILL, cols].astype(jnp.bfloat16)
        spill_down[d] = wide[SPILL + tile_rows :, cols].astype(jnp.bfloat16)
        return carry

    lax.fori_loop(0, n, emit, 0)
    start = pl.multiple_of(BLOCK + me[0] * tile_cols, BLOCK)
    own[...] = wide[SPILL : SPILL + tile_rows, pl.ds(start, tile_cols)]


def reduce_kernel(
    n, strips, bands, depth, matched, own, spill_up, spill_down, coadd, detection,
    moving, outgoing, incoming, spilled, det_mine, det_theirs,
    send_sem, recv_sem, match_send, match_recv,
    spill_send, spill_recv, det_send, det_recv,
):
    me = lax.axis_index("exp")
    strip = lax.axis_index("tile")
    band = lax.axis_index("band")
    rows_all = depth.shape[1]
    chunk = 32
    barrier = pltpu.get_barrier_semaphore()
    greet = [
        (strip > 0, {"tile": strip - 1}),
        (strip < strips - 1, {"tile": strip + 1}),
    ]
    for here, peer in greet:

        @pl.when(here)
        def _(peer=peer):
            pl.semaphore_signal(barrier, inc=1, device_id=peer, device_id_type=MESH)

    for j in range(1, n):
        pl.semaphore_signal(
            barrier, inc=1, device_id={"exp": lax.rem(me + j, n)}, device_id_type=MESH
        )
    for j in range(1, bands):
        pl.semaphore_signal(
            barrier, inc=1, device_id={"band": lax.rem(band + j, bands)}, device_id_type=MESH
        )
    peers = bands - 1 + n - 1
    for here, _peer in greet:
        peers = peers + here.astype(jnp.int32)
    pl.semaphore_wait(barrier, peers)

    def spill_copy(side):
        peer = strip + 1 if side == 0 else strip - 1
        return pltpu.make_async_remote_copy(
            src_ref=spill_down if side == 0 else spill_up,
            dst_ref=spilled.at[side],
            send_sem=spill_send.at[side],
            recv_sem=spill_recv.at[side],
            device_id={"tile": peer},
            device_id_type=MESH,
        )

    sends_spill = (strip < strips - 1, strip > 0)
    gets_spill = (strip > 0, strip < strips - 1)
    for side in range(2):

        @pl.when(sends_spill[side])
        def _(side=side):
            spill_copy(side).start()

        @pl.when(jnp.logical_not(gets_spill[side]))
        def _(side=side):
            spilled[side] = jnp.zeros(spilled.shape[1:], spilled.dtype)

    def unit_copy(d, right):
        place = d if right else jnp.where(d == me - 1, n, d)
        return pltpu.make_async_remote_copy(
            src_ref=moving.at[d],
            dst_ref=moving.at[place],
            send_sem=send_sem.at[d],
            recv_sem=recv_sem.at[place],
            device_id={"exp": me + 1 if right else me - 1},
            device_id_type=MESH,
        )

    def arrived(place):
        pltpu.make_async_remote_copy(
            src_ref=moving.at[place],
            dst_ref=moving.at[place],
            send_sem=send_sem.at[0],
            recv_sem=recv_sem.at[place],
            device_id={"band": lax.rem(band + 1, bands)},
            device_id_type=MESH,
        ).wait_recv()

    def pass_on(d, right, gets):
        @pl.when(gets)
        def _():
            arrived(d)
            for r in range(0, rows_all, chunk):
                rows = slice(r, r + chunk)
                moving[d, rows] = (
                    moving[d, rows].astype(jnp.float32) + depth[d, rows].astype(jnp.float32)
                ).astype(jnp.bfloat16)

        @pl.when(jnp.logical_not(gets))
        def _():
            for r in range(0, rows_all, chunk):
                moving[d, r : r + chunk] = depth[d, r : r + chunk]

        unit_copy(d, right).start()

    def match_copy(j):
        return pltpu.make_async_remote_copy(
            src_ref=outgoing.at[j],
            dst_ref=incoming.at[j],
            send_sem=match_send.at[j],
            recv_sem=match_recv.at[j],
            device_id={"exp": lax.rem(me + j, n)},
            device_id_type=MESH,
        )

    def edges(d, r):
        value = None
        if r < SPILL:
            value = spilled[0, d, r : r + chunk].astype(jnp.float32)
        if r >= rows_all - SPILL:
            low = r - (rows_all - SPILL)
            value = spilled[1, d, low : low + chunk].astype(jnp.float32)
        return value

    def step_depth(gets_now):
        def step(s, carry):
            to_right = n - 1 - s

            @pl.when((to_right > me) & ((me > 0) == gets_now))
            def _():
                pass_on(to_right, True, me > 0)

            @pl.when((s < me) & ((me < n - 1) == gets_now))
            def _():
                pass_on(s, False, me < n - 1)

            return carry

        lax.fori_loop(0, n - 1, step, 0)

    step_depth(False)
    for side in range(2):

        @pl.when(gets_spill[side])
        def _(side=side):
            spill_copy(side).wait_recv()

    def send_match(i, carry):
        j = n - 1 - i
        d = lax.rem(me + j, n)
        for r in range(0, rows_all, chunk):
            rows = slice(r, r + chunk)
            edge = edges(d, r)
            if edge is None:
                outgoing[j, rows] = matched[d, rows]
            else:
                outgoing[j, rows] = (matched[d, rows].astype(jnp.float32) + edge).astype(
                    jnp.bfloat16
                )
        match_copy(j).start()
        return carry

    lax.fori_loop(0, n - 1, send_match, 0)
    step_depth(True)

    @pl.when(me > 0)
    def _():
        arrived(me)

    @pl.when(me == 0)
    def _():
        moving[me] = jnp.zeros(moving.shape[1:], moving.dtype)

    @pl.when(me < n - 1)
    def _():
        arrived(n)

    @pl.when(me == n - 1)
    def _():
        moving[n] = jnp.zeros(moving.shape[1:], moving.dtype)

    for r in range(0, rows_all, chunk):
        rows = slice(r, r + chunk)
        edge = edges(me, r)
        coadd[rows] = own[rows] if edge is None else own[rows] + edge

    def gather(i, carry):
        j = i + 1
        match_copy(j).wait_recv()
        for r in range(0, rows_all, chunk):
            rows = slice(r, r + chunk)
            coadd[rows] += incoming[j, rows].astype(jnp.float32)
        return carry

    lax.fori_loop(0, n - 1, gather, 0)
    for r in range(0, rows_all, chunk):
        rows = slice(r, r + chunk)
        denominator = 1.0 + (
            depth[me, rows].astype(jnp.float32)
            + moving[me, rows].astype(jnp.float32)
            + moving[n, rows].astype(jnp.float32)
        )
        value = coadd[rows] / denominator
        coadd[rows] = value
        det_mine[rows] = value * value * denominator

    def det_copy(j):
        return pltpu.make_async_remote_copy(
            src_ref=det_mine,
            dst_ref=det_theirs.at[j - 1],
            send_sem=det_send.at[j - 1],
            recv_sem=det_recv.at[j - 1],
            device_id={"band": lax.rem(band + j, bands)},
            device_id_type=MESH,
        )

    for j in range(1, bands):
        det_copy(j).start()
    for j in range(1, bands):
        det_copy(j).wait()
    for r in range(0, rows_all, chunk):
        rows = slice(r, r + chunk)
        value = det_mine[rows]
        for j in range(1, bands):
            value += det_theirs[j - 1, rows]
        detection[rows] = value

    def drain(s, carry):
        to_right = n - 1 - s
        match_copy(s + 1).wait_send()

        @pl.when(to_right > me)
        def _():
            unit_copy(to_right, True).wait_send()

        @pl.when(s < me)
        def _():
            unit_copy(s, False).wait_send()

        return carry

    lax.fori_loop(0, n - 1, drain, 0)
    for side in range(2):

        @pl.when(sends_spill[side])
        def _(side=side):
            spill_copy(side).wait_send()


def local(sizes, images, mask_bits, inv_var, routes, block_slot, kernel_index, coefficients):
    n, strips, bands = sizes["exp"], sizes["tile"], sizes["band"]
    held = images.shape[2]
    tile_rows = BLOCK_ROWS * BLOCK
    tile_cols = BLOCK_COLS * BLOCK
    half = tile_cols // 2
    across = tap_pair(tap_matrix(2 * half, half, BLOCK))
    down = tap_pair(tap_matrix(tile_rows + 2 * SPILL, tile_rows, SPILL))
    smem = pl.BlockSpec(memory_space=pltpu.SMEM)
    vmem = pl.BlockSpec(memory_space=pltpu.VMEM)
    plane = jax.ShapeDtypeStruct((n, tile_rows, tile_cols), jnp.bfloat16)
    spill = jax.ShapeDtypeStruct((n, SPILL, tile_cols), jnp.bfloat16)
    whole = jax.ShapeDtypeStruct((tile_rows, tile_cols), jnp.float32)
    placed = pl.pallas_call(
        functools.partial(place_kernel, n, held),
        out_shape=(plane, plane, whole, spill, spill),
        in_specs=[smem] * 6 + [vmem] * 4,
        out_specs=(vmem,) * 5,
        scratch_shapes=[
            pltpu.VMEM((4, tile_rows, tile_cols), jnp.float32),
            pltpu.VMEM((tile_rows + 2 * SPILL, n * tile_cols + 2 * BLOCK), jnp.float32),
        ],
        name="place_and_match",
    )(
        lax.axis_index("exp").reshape(1), routes[0, 0, :, 0], block_slot[0, 0],
        kernel_index[0, 0], inv_var[0, 0], coefficients, images[0, 0], mask_bits[0, 0],
        across, down,
    )
    coadd, detection = pl.pallas_call(
        functools.partial(reduce_kernel, n, strips, bands),
        out_shape=(whole, whole),
        in_specs=[vmem] * 5,
        out_specs=(vmem, vmem),
        scratch_shapes=[
            pltpu.VMEM((n + 1, tile_rows, tile_cols), jnp.bfloat16),
            pltpu.VMEM((n, tile_rows, tile_cols), jnp.bfloat16),
            pltpu.VMEM((n, tile_rows, tile_cols), jnp.bfloat16),
            pltpu.VMEM((2, n, SPILL, tile_cols), jnp.bfloat16),
            pltpu.VMEM((tile_rows, tile_cols), jnp.float32),
            pltpu.VMEM((bands - 1, tile_rows, tile_cols), jnp.float32),
            pltpu.SemaphoreType.DMA((n,)),
            pltpu.SemaphoreType.DMA((n + 1,)),
            pltpu.SemaphoreType.DMA((n,)),
            pltpu.SemaphoreType.DMA((n,)),
            pltpu.SemaphoreType.DMA((2,)),
            pltpu.SemaphoreType.DMA((2,)),
            pltpu.SemaphoreType.DMA((bands - 1,)),
            pltpu.SemaphoreType.DMA((bands - 1,)),
        ],
        compiler_params=pltpu.CompilerParams(collective_id=0, has_side_effects=True),
        name="reduce_and_finish",
    )(*placed)
    return coadd[None], detection


def solution(mesh):
    return jax.shard_map(
        functools.partial(local, dict(mesh.shape)),
        mesh=mesh,
        in_specs=(
            P(("patch", "band"), "tile", "exp", None, None),
            P(("patch", "band"), "tile", "exp", None, None),
            P(("patch", "band"), "tile", "exp"),
            P(("patch", "band"), "tile", "exp", None),
            P(("patch", "band"), "tile", "exp"),
            P(("patch", "band"), "tile", "exp"),
            P(),
        ),
        out_specs=(P(("patch", "band"), "tile", "exp"), P(("patch", "tile"), "exp")),
        check_vma=False,
    )
```

```python
import functools

import jax
import jax.numpy as jnp
import numpy as np
from jax import lax
from jax.experimental import pallas as pl
from jax.experimental.pallas import tpu as pltpu
from jax.sharding import PartitionSpec as P

BLOCK = 128
TAPS = 41
BLOCK_ROWS = 2
BLOCK_COLS = 4
SPILL = 32

kernel_sigmas = (1.0, 2.5, 6.0)
MESH = pl.DeviceIdType.MESH


def tap_matrix(rows, cols, shift):
    half_span = TAPS // 2
    offset = np.arange(rows)[:, None] - np.arange(cols)[None, :] - shift
    axis = np.arange(-half_span, half_span + 1).astype(np.float64)
    result = []
    for spread in kernel_sigmas:
        norm = np.sum(np.exp(-axis * axis / (2.0 * spread * spread)))
        result.append(
            np.where(
                np.abs(offset) <= half_span,
                np.exp(-offset * offset / (2.0 * spread * spread)),
                0.0,
            )
            / norm
        )
    return np.stack(result)


def tap_pair(taps):
    high = taps.astype(jnp.bfloat16)
    low = (taps - high.astype(np.float64)).astype(jnp.bfloat16)
    return jnp.asarray(np.stack([high, low]))


def split(value):
    high = value.astype(jnp.bfloat16)
    return high, (value - high.astype(jnp.float32)).astype(jnp.bfloat16)


def dot3(left, right):
    (left_high, left_low), (right_high, right_low) = left, right
    dot = functools.partial(jnp.dot, preferred_element_type=jnp.float32)
    return dot(left_high, right_high) + (dot(left_high, right_low) + dot(left_low, right_high))


def place_kernel(
    held, routes, slots, kernels, inverse, coefs, images, masks, depth, basis, acc
):
    d = pl.program_id(0)
    acc[...] = jnp.zeros_like(acc)

    def one(i, carry):
        @pl.when(routes[i] == d)
        def _():
            slot = slots[i]
            which = kernels[i]
            rows = pl.ds(pl.multiple_of(slot // BLOCK_COLS * BLOCK, BLOCK), BLOCK)
            cols = pl.ds(pl.multiple_of(slot % BLOCK_COLS * BLOCK, BLOCK), BLOCK)
            bits = masks[i]
            suspect = jnp.bitwise_and(bits, 1).astype(jnp.float32)
            usable = jnp.where(jnp.bitwise_and(bits, 6) == 6, 0.0, 1.0 - 0.5 * suspect)
            scaled = usable * inverse[i]
            weighted = (
                (scaled * images[i].astype(jnp.float32)).astype(jnp.bfloat16).astype(jnp.float32)
            )
            weight = scaled.astype(jnp.bfloat16).astype(jnp.float32)
            for k in range(3):
                acc[k, rows, cols] += coefs[k, which] * weighted
            acc[3, rows, cols] += weight

        return carry

    lax.fori_loop(0, held, one, 0)
    depth[0] = acc[3].astype(jnp.bfloat16)
    for k in range(3):
        basis[0, 0, k], basis[0, 1, k] = split(acc[k])


def reduce_kernel(
    n, strips, bands, depth, basis, across, down, numerator, denominator, det_mine, det_theirs,
    moving, outgoing, incoming, framed, result, spilling, spilled,
    send_sem, recv_sem, match_send, match_recv,
    spill_send, spill_recv, det_send, det_recv, frame_sem,
):
    me = lax.axis_index("exp")
    strip = lax.axis_index("tile")
    band = lax.axis_index("band")
    rows_all = depth.shape[1]
    chunk = 32
    barrier = pltpu.get_barrier_semaphore()
    greet = [
        (strip > 0, {"tile": strip - 1}),
        (strip < strips - 1, {"tile": strip + 1}),
    ]
    for here, peer in greet:

        @pl.when(here)
        def _(peer=peer):
            pl.semaphore_signal(barrier, inc=1, device_id=peer, device_id_type=MESH)

    for j in range(1, n):
        pl.semaphore_signal(
            barrier, inc=1, device_id={"exp": lax.rem(me + j, n)}, device_id_type=MESH
        )
    for j in range(1, bands):
        pl.semaphore_signal(
            barrier, inc=1, device_id={"band": lax.rem(band + j, bands)}, device_id_type=MESH
        )
    peers = bands - 1 + n - 1
    for here, _peer in greet:
        peers = peers + here.astype(jnp.int32)
    pl.semaphore_wait(barrier, peers)

    tile_cols = depth.shape[2]
    half = tile_cols // 2

    def frame_copies(j, slot):
        d = lax.rem(me + j, n)
        before = jnp.maximum(d - 1, 0)
        after = jnp.minimum(d + 1, n - 1)
        whole = pl.ds(BLOCK, tile_cols)
        return (
            pltpu.make_async_copy(
                basis.at[d], framed.at[slot, :, :, :, whole], frame_sem.at[slot, 0]
            ),
            pltpu.make_async_copy(
                basis.at[before, :, :, :, pl.ds(tile_cols - BLOCK, BLOCK)],
                framed.at[slot, :, :, :, pl.ds(0, BLOCK)],
                frame_sem.at[slot, 1],
            ),
            pltpu.make_async_copy(
                basis.at[after, :, :, :, pl.ds(0, BLOCK)],
                framed.at[slot, :, :, :, pl.ds(BLOCK + tile_cols, BLOCK)],
                frame_sem.at[slot, 2],
            ),
        )

    def spill_copy(side, j):
        peer = strip + 1 if side == 0 else strip - 1
        return pltpu.make_async_remote_copy(
            src_ref=spilling.at[side, j],
            dst_ref=spilled.at[side, j],
            send_sem=spill_send.at[side, j],
            recv_sem=spill_recv.at[side, j],
            device_id={"tile": peer},
            device_id_type=MESH,
        )

    sends_spill = (strip < strips - 1, strip > 0)
    gets_spill = (strip > 0, strip < strips - 1)
    for side in range(2):

        @pl.when(jnp.logical_not(gets_spill[side]))
        def _(side=side):
            spilled[side] = jnp.zeros(spilled.shape[1:], spilled.dtype)

    def correlate(j, slot):
        d = lax.rem(me + j, n)
        for copy in frame_copies(j, slot):
            copy.wait()

        @pl.when(d == 0)
        def _():
            framed[slot, :, :, :, 0:BLOCK] = jnp.zeros(
                framed.shape[1:4] + (BLOCK,), framed.dtype
            )

        @pl.when(d == n - 1)
        def _():
            framed[slot, :, :, :, BLOCK + tile_cols :] = jnp.zeros(
                framed.shape[1:4] + (BLOCK,), framed.dtype
            )

        for h in range(2):
            total = None
            for k in range(3):
                cols = slice(h * half, h * half + half + 2 * BLOCK)
                tall = dot3(
                    (down[0, k], down[1, k]),
                    (framed[slot, 0, k, :, cols], framed[slot, 1, k, :, cols]),
                )
                term = dot3(split(tall), (across[0, k], across[1, k]))
                total = term if total is None else total + term
            out = slice(h * half, (h + 1) * half)
            result[slot, :, out] = total[SPILL : SPILL + rows_all]
            spilling[0, j, :, out] = total[SPILL + rows_all :].astype(jnp.bfloat16)
            spilling[1, j, :, out] = total[0:SPILL].astype(jnp.bfloat16)
        for side in range(2):

            @pl.when(sends_spill[side])
            def _(side=side):
                spill_copy(side, j).start()

    def unit_copy(d, right):
        place = d if right else jnp.where(d == me - 1, n, d)
        return pltpu.make_async_remote_copy(
            src_ref=moving.at[d],
            dst_ref=moving.at[place],
            send_sem=send_sem.at[d],
            recv_sem=recv_sem.at[place],
            device_id={"exp": me + 1 if right else me - 1},
            device_id_type=MESH,
        )

    def arrived(place):
        pltpu.make_async_remote_copy(
            src_ref=moving.at[place],
            dst_ref=moving.at[place],
            send_sem=send_sem.at[0],
            recv_sem=recv_sem.at[place],
            device_id={"band": lax.rem(band + 1, bands)},
            device_id_type=MESH,
        ).wait_recv()

    def pass_on(d, right, gets):
        @pl.when(gets)
        def _():
            arrived(d)
            for r in range(0, rows_all, chunk):
                rows = slice(r, r + chunk)
                moving[d, rows] = (
                    moving[d, rows].astype(jnp.float32) + depth[d, rows].astype(jnp.float32)
                ).astype(jnp.bfloat16)

        @pl.when(jnp.logical_not(gets))
        def _():
            for r in range(0, rows_all, chunk):
                moving[d, r : r + chunk] = depth[d, r : r + chunk]

        unit_copy(d, right).start()

    def match_copy(j):
        return pltpu.make_async_remote_copy(
            src_ref=outgoing.at[j],
            dst_ref=incoming.at[j],
            send_sem=match_send.at[j],
            recv_sem=match_recv.at[j],
            device_id={"exp": lax.rem(me + j, n)},
            device_id_type=MESH,
        )

    def edges(j, r):
        value = None
        if r < SPILL:
            value = spilled[0, j, r : r + chunk].astype(jnp.float32)
        if r >= rows_all - SPILL:
            low = r - (rows_all - SPILL)
            value = spilled[1, j, low : low + chunk].astype(jnp.float32)
        return value

    def complete(j, slot):
        for side in range(2):

            @pl.when(gets_spill[side])
            def _(side=side):
                spill_copy(side, j).wait_recv()

        for r in range(0, rows_all, chunk):
            rows = slice(r, r + chunk)
            edge = edges(j, r)
            value = result[slot, rows]
            if edge is not None:
                value += edge
            if isinstance(j, int):
                numerator[rows] = value
            else:
                outgoing[j, rows] = value.astype(jnp.bfloat16)

    def step_right(s, carry):
        @pl.when(n - 1 - s > me)
        def _():
            pass_on(n - 1 - s, True, me > 0)

        return carry

    def step_left(s, carry):
        @pl.when(s < me)
        def _():
            pass_on(s, False, me < n - 1)

        return carry

    for copy in frame_copies(n - 1, 0):
        copy.start()

    @pl.when(me == 0)
    def _():
        lax.fori_loop(0, n - 1, step_right, 0)

    @pl.when(me == n - 1)
    def _():
        lax.fori_loop(0, n - 1, step_left, 0)

    def turn(i, carry):
        j = n - 1 - i
        slot = lax.rem(i, 2)

        @pl.when(i < n - 1)
        def _():
            for copy in frame_copies(j - 1, 1 - slot):
                copy.start()

        correlate(j, slot)

        @pl.when(i > 0)
        def _():
            complete(j + 1, 1 - slot)
            match_copy(j + 1).start()

        return carry

    lax.fori_loop(0, n, turn, 0)
    complete(0, (n - 1) % 2)

    right_first = 2 * me < n - 1

    @pl.when(right_first & (me > 0))
    def _():
        lax.fori_loop(0, n - 1, step_right, 0)

    @pl.when(me < n - 1)
    def _():
        lax.fori_loop(0, n - 1, step_left, 0)

    @pl.when(jnp.logical_not(right_first) & (me > 0))
    def _():
        lax.fori_loop(0, n - 1, step_right, 0)

    @pl.when(me > 0)
    def _():
        arrived(me)

    @pl.when(me == 0)
    def _():
        moving[me] = jnp.zeros(moving.shape[1:], moving.dtype)

    @pl.when(me < n - 1)
    def _():
        arrived(n)

    @pl.when(me == n - 1)
    def _():
        moving[n] = jnp.zeros(moving.shape[1:], moving.dtype)

    def gather(i, carry):
        j = i + 1
        match_copy(j).wait_recv()
        for r in range(0, rows_all, chunk):
            rows = slice(r, r + chunk)
            numerator[rows] += incoming[j, rows].astype(jnp.float32)
        return carry

    lax.fori_loop(0, n - 1, gather, 0)
    for r in range(0, rows_all, chunk):
        rows = slice(r, r + chunk)
        below = 1.0 + (
            depth[me, rows].astype(jnp.float32)
            + moving[me, rows].astype(jnp.float32)
            + moving[n, rows].astype(jnp.float32)
        )
        denominator[rows] = below
        value = numerator[rows] / below
        det_mine[rows] = value * value * below

    def det_copy(j):
        return pltpu.make_async_remote_copy(
            src_ref=det_mine,
            dst_ref=det_theirs.at[j - 1],
            send_sem=det_send.at[j - 1],
            recv_sem=det_recv.at[j - 1],
            device_id={"band": lax.rem(band + j, bands)},
            device_id_type=MESH,
        )

    for j in range(1, bands):
        det_copy(j).start()
    for j in range(1, bands):
        det_copy(j).wait()

    def drain(s, carry):
        to_right = n - 1 - s
        match_copy(s + 1).wait_send()

        @pl.when(to_right > me)
        def _():
            unit_copy(to_right, True).wait_send()

        @pl.when(s < me)
        def _():
            unit_copy(s, False).wait_send()

        return carry

    lax.fori_loop(0, n - 1, drain, 0)

    def drain_spill(j, carry):
        for side in range(2):

            @pl.when(sends_spill[side])
            def _(side=side):
                spill_copy(side, j).wait_send()

        return carry

    lax.fori_loop(0, n, drain_spill, 0)


def local(sizes, images, mask_bits, inv_var, routes, block_slot, kernel_index, coefficients):
    n, strips, bands = sizes["exp"], sizes["tile"], sizes["band"]
    held = images.shape[2]
    tile_rows = BLOCK_ROWS * BLOCK
    tile_cols = BLOCK_COLS * BLOCK
    half = tile_cols // 2
    across = tap_pair(tap_matrix(2 * half, half, BLOCK))
    down = tap_pair(tap_matrix(tile_rows + 2 * SPILL, tile_rows, SPILL))
    smem = pl.BlockSpec(memory_space=pltpu.SMEM)
    vmem = pl.BlockSpec(memory_space=pltpu.VMEM)
    depth, basis = pl.pallas_call(
        functools.partial(place_kernel, held),
        grid=(n,),
        out_shape=(
            jax.ShapeDtypeStruct((n, tile_rows, tile_cols), jnp.bfloat16),
            jax.ShapeDtypeStruct((n, 2, 3, tile_rows, tile_cols), jnp.bfloat16),
        ),
        in_specs=[smem] * 5 + [vmem] * 2,
        out_specs=(
            pl.BlockSpec((1, tile_rows, tile_cols), lambda d: (d, 0, 0)),
            pl.BlockSpec((1, 2, 3, tile_rows, tile_cols), lambda d: (d, 0, 0, 0, 0)),
        ),
        scratch_shapes=[pltpu.VMEM((4, tile_rows, tile_cols), jnp.float32)],
        name="place",
    )(
        routes[0, 0, :, 0], block_slot[0, 0], kernel_index[0, 0], inv_var[0, 0],
        coefficients.T, images[0, 0], mask_bits[0, 0],
    )
    whole = jax.ShapeDtypeStruct((tile_rows, tile_cols), jnp.float32)
    others = jax.ShapeDtypeStruct((bands - 1, tile_rows, tile_cols), jnp.float32)
    numerator, denominator, det_mine, det_theirs = pl.pallas_call(
        functools.partial(reduce_kernel, n, strips, bands),
        out_shape=(whole, whole, whole, others),
        in_specs=[vmem, pl.BlockSpec(memory_space=pl.ANY), vmem, vmem],
        out_specs=(vmem,) * 4,
        scratch_shapes=[
            pltpu.VMEM((n + 1, tile_rows, tile_cols), jnp.bfloat16),
            pltpu.VMEM((n, tile_rows, tile_cols), jnp.bfloat16),
            pltpu.VMEM((n, tile_rows, tile_cols), jnp.bfloat16),
            pltpu.VMEM((2, 2, 3, tile_rows, tile_cols + 2 * BLOCK), jnp.bfloat16),
            pltpu.VMEM((2, tile_rows, tile_cols), jnp.float32),
            pltpu.VMEM((2, n, SPILL, tile_cols), jnp.bfloat16),
            pltpu.VMEM((2, n, SPILL, tile_cols), jnp.bfloat16),
            pltpu.SemaphoreType.DMA((n,)),
            pltpu.SemaphoreType.DMA((n + 1,)),
            pltpu.SemaphoreType.DMA((n,)),
            pltpu.SemaphoreType.DMA((n,)),
            pltpu.SemaphoreType.DMA((2, n)),
            pltpu.SemaphoreType.DMA((2, n)),
            pltpu.SemaphoreType.DMA((bands - 1,)),
            pltpu.SemaphoreType.DMA((bands - 1,)),
            pltpu.SemaphoreType.DMA((2, 3)),
        ],
        compiler_params=pltpu.CompilerParams(collective_id=0, has_side_effects=True),
        name="correlate_and_reduce",
    )(depth, basis, across, down)
    return (numerator / denominator)[None], det_mine + jnp.sum(det_theirs, axis=0)


def solution(mesh):
    return jax.shard_map(
        functools.partial(local, dict(mesh.shape)),
        mesh=mesh,
        in_specs=(
            P(("patch", "band"), "tile", "exp", None, None),
            P(("patch", "band"), "tile", "exp", None, None),
            P(("patch", "band"), "tile", "exp"),
            P(("patch", "band"), "tile", "exp", None),
            P(("patch", "band"), "tile", "exp"),
            P(("patch", "band"), "tile", "exp"),
            P(),
        ),
        out_specs=(P(("patch", "band"), "tile", "exp"), P(("patch", "tile"), "exp")),
        check_vma=False,
    )
```

```python
import functools

import jax
import jax.numpy as jnp
import numpy as np
from jax import lax
from jax.experimental import pallas as pl
from jax.experimental.pallas import tpu as pltpu
from jax.sharding import PartitionSpec as P

BLOCK = 128
TAPS = 41
BLOCK_ROWS = 2
BLOCK_COLS = 4
SPILL = 24

kernel_sigmas = (1.0, 2.5, 6.0)
MESH = pl.DeviceIdType.MESH


def tap_matrix(rows, cols, shift):
    half_span = TAPS // 2
    offset = np.arange(rows)[:, None] - np.arange(cols)[None, :] - shift
    axis = np.arange(-half_span, half_span + 1).astype(np.float64)
    result = []
    for spread in kernel_sigmas:
        norm = np.sum(np.exp(-axis * axis / (2.0 * spread * spread)))
        result.append(
            np.where(
                np.abs(offset) <= half_span,
                np.exp(-offset * offset / (2.0 * spread * spread)),
                0.0,
            )
            / norm
        )
    return np.stack(result)


def tap_pair(taps):
    high = taps.astype(jnp.bfloat16)
    low = (taps - high.astype(np.float64)).astype(jnp.bfloat16)
    return jnp.asarray(np.stack([high, low]))


def split(value):
    high = value.astype(jnp.bfloat16)
    return high, (value - high.astype(jnp.float32)).astype(jnp.bfloat16)


def products(pairs):
    total = None
    for left, right in pairs:
        term = jnp.dot(left, right, preferred_element_type=jnp.float32)
        total = term if total is None else total + term
    return total


def place_kernel(
    held, routes, slots, kernels, inverse, coefs, images, masks, depth, basis, acc
):
    d = pl.program_id(0)
    acc[...] = jnp.zeros_like(acc)

    def one(i, carry):
        @pl.when(routes[i] == d)
        def _():
            slot = slots[i]
            which = kernels[i]
            rows = pl.ds(pl.multiple_of(slot // BLOCK_COLS * BLOCK, BLOCK), BLOCK)
            cols = pl.ds(pl.multiple_of(slot % BLOCK_COLS * BLOCK, BLOCK), BLOCK)
            bits = masks[i]
            suspect = jnp.bitwise_and(bits, 1).astype(jnp.float32)
            usable = jnp.where(jnp.bitwise_and(bits, 6) == 6, 0.0, 1.0 - 0.5 * suspect)
            scaled = usable * inverse[i]
            weighted = (
                (scaled * images[i].astype(jnp.float32)).astype(jnp.bfloat16).astype(jnp.float32)
            )
            weight = scaled.astype(jnp.bfloat16).astype(jnp.float32)
            for k in range(3):
                acc[k, rows, cols] += coefs[k, which] * weighted
            acc[3, rows, cols] += weight

        return carry

    lax.fori_loop(0, held, one, 0)
    depth[0] = acc[3].astype(jnp.bfloat16)
    basis[0, 0], basis[0, 1] = split(acc[0])
    basis[0, 2] = acc[1].astype(jnp.bfloat16)
    basis[0, 3] = acc[2].astype(jnp.bfloat16)


def reduce_kernel(
    n, strips, bands, depth, basis, across, down, numerator, denominator, det_mine, det_theirs,
    moving, outgoing, incoming, framed, result, spilling, spilled,
    send_sem, recv_sem, match_send, match_recv,
    spill_send, spill_recv, det_send, det_recv, frame_sem,
):
    me = lax.axis_index("exp")
    strip = lax.axis_index("tile")
    band = lax.axis_index("band")
    rows_all = depth.shape[1]
    chunk = 32
    barrier = pltpu.get_barrier_semaphore()
    greet = [
        (strip > 0, {"tile": strip - 1}),
        (strip < strips - 1, {"tile": strip + 1}),
    ]
    for here, peer in greet:

        @pl.when(here)
        def _(peer=peer):
            pl.semaphore_signal(barrier, inc=1, device_id=peer, device_id_type=MESH)

    for j in range(1, n):
        pl.semaphore_signal(
            barrier, inc=1, device_id={"exp": lax.rem(me + j, n)}, device_id_type=MESH
        )
    for j in range(1, bands):
        pl.semaphore_signal(
            barrier, inc=1, device_id={"band": lax.rem(band + j, bands)}, device_id_type=MESH
        )
    peers = bands - 1 + n - 1
    for here, _peer in greet:
        peers = peers + here.astype(jnp.int32)
    pl.semaphore_wait(barrier, peers)

    tile_cols = depth.shape[2]
    half = tile_cols // 2

    def frame_copies(j, slot):
        d = lax.rem(me + j, n)
        before = jnp.maximum(d - 1, 0)
        after = jnp.minimum(d + 1, n - 1)
        whole = pl.ds(BLOCK, tile_cols)
        return (
            pltpu.make_async_copy(
                basis.at[d], framed.at[slot, :, :, whole], frame_sem.at[slot, 0]
            ),
            pltpu.make_async_copy(
                basis.at[before, :, :, pl.ds(tile_cols - BLOCK, BLOCK)],
                framed.at[slot, :, :, pl.ds(0, BLOCK)],
                frame_sem.at[slot, 1],
            ),
            pltpu.make_async_copy(
                basis.at[after, :, :, pl.ds(0, BLOCK)],
                framed.at[slot, :, :, pl.ds(BLOCK + tile_cols, BLOCK)],
                frame_sem.at[slot, 2],
            ),
        )

    def spill_copy(side, j):
        peer = strip + 1 if side == 0 else strip - 1
        return pltpu.make_async_remote_copy(
            src_ref=spilling.at[side, j],
            dst_ref=spilled.at[side, j],
            send_sem=spill_send.at[side, j],
            recv_sem=spill_recv.at[side, j],
            device_id={"tile": peer},
            device_id_type=MESH,
        )

    sends_spill = (strip < strips - 1, strip > 0)
    gets_spill = (strip > 0, strip < strips - 1)
    for side in range(2):

        @pl.when(jnp.logical_not(gets_spill[side]))
        def _(side=side):
            spilled[side] = jnp.zeros(spilled.shape[1:], spilled.dtype)

    def correlate(j, slot):
        d = lax.rem(me + j, n)
        for copy in frame_copies(j, slot):
            copy.wait()

        @pl.when(d == 0)
        def _():
            framed[slot, :, :, 0:BLOCK] = jnp.zeros(
                framed.shape[1:3] + (BLOCK,), framed.dtype
            )

        @pl.when(d == n - 1)
        def _():
            framed[slot, :, :, BLOCK + tile_cols :] = jnp.zeros(
                framed.shape[1:3] + (BLOCK,), framed.dtype
            )

        first = (framed[slot, 0], framed[slot, 1])
        tall_high, tall_low = split(
            products(((down[0, 0], first[0]), (down[0, 0], first[1]), (down[1, 0], first[0])))
        )
        second = framed[slot, 2]
        tall_second = products(((down[0, 1], second), (down[1, 1], second))).astype(jnp.bfloat16)
        tall_third = products(((down[0, 2], framed[slot, 3]),)).astype(jnp.bfloat16)
        for h in range(2):
            cols = slice(h * half, h * half + half + 2 * BLOCK)
            total = products((
                (tall_high[:, cols], across[0, 0]),
                (tall_high[:, cols], across[1, 0]),
                (tall_low[:, cols], across[0, 0]),
                (tall_second[:, cols], across[0, 1]),
                (tall_second[:, cols], across[1, 1]),
                (tall_third[:, cols], across[0, 2]),
            ))
            out = slice(h * half, (h + 1) * half)
            result[slot, :, out] = total[SPILL : SPILL + rows_all]
            spilling[0, j, :, out] = total[SPILL + rows_all :].astype(jnp.bfloat16)
            spilling[1, j, :, out] = total[0:SPILL].astype(jnp.bfloat16)
        for side in range(2):

            @pl.when(sends_spill[side])
            def _(side=side):
                spill_copy(side, j).start()

    def unit_copy(d, right):
        place = d if right else jnp.where(d == me - 1, n, d)
        return pltpu.make_async_remote_copy(
            src_ref=moving.at[d],
            dst_ref=moving.at[place],
            send_sem=send_sem.at[d],
            recv_sem=recv_sem.at[place],
            device_id={"exp": me + 1 if right else me - 1},
            device_id_type=MESH,
        )

    def arrived(place):
        pltpu.make_async_remote_copy(
            src_ref=moving.at[place],
            dst_ref=moving.at[place],
            send_sem=send_sem.at[0],
            recv_sem=recv_sem.at[place],
            device_id={"band": lax.rem(band + 1, bands)},
            device_id_type=MESH,
        ).wait_recv()

    def pass_on(d, right, gets):
        @pl.when(gets)
        def _():
            arrived(d)
            for r in range(0, rows_all, chunk):
                rows = slice(r, r + chunk)
                moving[d, rows] = (
                    moving[d, rows].astype(jnp.float32) + depth[d, rows].astype(jnp.float32)
                ).astype(jnp.bfloat16)

        @pl.when(jnp.logical_not(gets))
        def _():
            for r in range(0, rows_all, chunk):
                moving[d, r : r + chunk] = depth[d, r : r + chunk]

        unit_copy(d, right).start()

    def match_copy(j):
        return pltpu.make_async_remote_copy(
            src_ref=outgoing.at[j],
            dst_ref=incoming.at[j],
            send_sem=match_send.at[j],
            recv_sem=match_recv.at[j],
            device_id={"exp": lax.rem(me + j, n)},
            device_id_type=MESH,
        )

    def complete(j, slot):
        for side in range(2):

            @pl.when(gets_spill[side])
            def _(side=side):
                spill_copy(side, j).wait_recv()

        low = rows_all - SPILL
        result[slot, 0:SPILL] += spilled[0, j].astype(jnp.float32)
        result[slot, low:] += spilled[1, j].astype(jnp.float32)
        if isinstance(j, int):
            numerator[...] = result[slot]
        else:
            for r in range(0, rows_all, chunk):
                outgoing[j, r : r + chunk] = result[slot, r : r + chunk].astype(jnp.bfloat16)

    def step_right(s, carry):
        @pl.when(n - 1 - s > me)
        def _():
            pass_on(n - 1 - s, True, me > 0)

        return carry

    def step_left(s, carry):
        @pl.when(s < me)
        def _():
            pass_on(s, False, me < n - 1)

        return carry

    for copy in frame_copies(n - 1, 0):
        copy.start()

    @pl.when(me == 0)
    def _():
        lax.fori_loop(0, n - 1, step_right, 0)

    @pl.when(me == n - 1)
    def _():
        lax.fori_loop(0, n - 1, step_left, 0)

    right_first = 2 * me < n - 1
    left_first = jnp.logical_not(right_first)

    def turn(i, carry):
        j = n - 1 - i
        slot = lax.rem(i, 2)

        @pl.when(i < n - 1)
        def _():
            for copy in frame_copies(j - 1, 1 - slot):
                copy.start()

        correlate(j, slot)

        @pl.when(i > 0)
        def _():
            complete(j + 1, 1 - slot)
            match_copy(j + 1).start()

        @pl.when((i > 1) & right_first & (me > 0))
        def _():
            step_right(i - 2, 0)

        @pl.when((i > 1) & left_first & (me < n - 1))
        def _():
            step_left(i - 2, 0)

        return carry

    lax.fori_loop(0, n, turn, 0)
    complete(0, (n - 1) % 2)

    @pl.when(right_first)
    def _():
        @pl.when(me > 0)
        def _():
            lax.fori_loop(max(n - 2, 0), n - 1, step_right, 0)

        lax.fori_loop(0, n - 1, step_left, 0)

    @pl.when(left_first)
    def _():
        @pl.when(me < n - 1)
        def _():
            lax.fori_loop(max(n - 2, 0), n - 1, step_left, 0)

        lax.fori_loop(0, n - 1, step_right, 0)

    @pl.when(me > 0)
    def _():
        arrived(me)

    @pl.when(me == 0)
    def _():
        moving[me] = jnp.zeros(moving.shape[1:], moving.dtype)

    @pl.when(me < n - 1)
    def _():
        arrived(n)

    @pl.when(me == n - 1)
    def _():
        moving[n] = jnp.zeros(moving.shape[1:], moving.dtype)

    def gather(i, carry):
        j = i + 1
        match_copy(j).wait_recv()
        for r in range(0, rows_all, chunk):
            rows = slice(r, r + chunk)
            numerator[rows] += incoming[j, rows].astype(jnp.float32)
        return carry

    lax.fori_loop(0, n - 1, gather, 0)
    for r in range(0, rows_all, chunk):
        rows = slice(r, r + chunk)
        below = 1.0 + (
            depth[me, rows].astype(jnp.float32)
            + moving[me, rows].astype(jnp.float32)
            + moving[n, rows].astype(jnp.float32)
        )
        denominator[rows] = below
        value = numerator[rows] / below
        det_mine[rows] = value * value * below

    def det_copy(j):
        return pltpu.make_async_remote_copy(
            src_ref=det_mine,
            dst_ref=det_theirs.at[j - 1],
            send_sem=det_send.at[j - 1],
            recv_sem=det_recv.at[j - 1],
            device_id={"band": lax.rem(band + j, bands)},
            device_id_type=MESH,
        )

    for j in range(1, bands):
        det_copy(j).start()
    for j in range(1, bands):
        det_copy(j).wait()

    def drain(s, carry):
        to_right = n - 1 - s
        match_copy(s + 1).wait_send()

        @pl.when(to_right > me)
        def _():
            unit_copy(to_right, True).wait_send()

        @pl.when(s < me)
        def _():
            unit_copy(s, False).wait_send()

        return carry

    lax.fori_loop(0, n - 1, drain, 0)

    def drain_spill(j, carry):
        for side in range(2):

            @pl.when(sends_spill[side])
            def _(side=side):
                spill_copy(side, j).wait_send()

        return carry

    lax.fori_loop(0, n, drain_spill, 0)


def finish_kernel(numerator, denominator, det_mine, det_theirs, coadd, detection):
    coadd[...] = numerator[...] / denominator[...]
    value = det_mine[...]
    for j in range(det_theirs.shape[0]):
        value += det_theirs[j]
    detection[...] = value


def local(sizes, images, mask_bits, inv_var, routes, block_slot, kernel_index, coefficients):
    n, strips, bands = sizes["exp"], sizes["tile"], sizes["band"]
    held = images.shape[2]
    tile_rows = BLOCK_ROWS * BLOCK
    tile_cols = BLOCK_COLS * BLOCK
    half = tile_cols // 2
    across = tap_pair(tap_matrix(2 * half, half, BLOCK))
    down = tap_pair(tap_matrix(tile_rows + 2 * SPILL, tile_rows, SPILL))
    smem = pl.BlockSpec(memory_space=pltpu.SMEM)
    vmem = pl.BlockSpec(memory_space=pltpu.VMEM)
    depth, basis = pl.pallas_call(
        functools.partial(place_kernel, held),
        grid=(n,),
        out_shape=(
            jax.ShapeDtypeStruct((n, tile_rows, tile_cols), jnp.bfloat16),
            jax.ShapeDtypeStruct((n, 4, tile_rows, tile_cols), jnp.bfloat16),
        ),
        in_specs=[smem] * 5 + [vmem] * 2,
        out_specs=(
            pl.BlockSpec((1, tile_rows, tile_cols), lambda d: (d, 0, 0)),
            pl.BlockSpec((1, 4, tile_rows, tile_cols), lambda d: (d, 0, 0, 0)),
        ),
        scratch_shapes=[pltpu.VMEM((4, tile_rows, tile_cols), jnp.float32)],
        name="place",
    )(
        routes[0, 0, :, 0], block_slot[0, 0], kernel_index[0, 0], inv_var[0, 0],
        coefficients.T, images[0, 0], mask_bits[0, 0],
    )
    whole = jax.ShapeDtypeStruct((tile_rows, tile_cols), jnp.float32)
    others = jax.ShapeDtypeStruct((bands - 1, tile_rows, tile_cols), jnp.float32)
    numerator, denominator, det_mine, det_theirs = pl.pallas_call(
        functools.partial(reduce_kernel, n, strips, bands),
        out_shape=(whole, whole, whole, others),
        in_specs=[vmem, pl.BlockSpec(memory_space=pl.ANY), vmem, vmem],
        out_specs=(vmem,) * 4,
        scratch_shapes=[
            pltpu.VMEM((n + 1, tile_rows, tile_cols), jnp.bfloat16),
            pltpu.VMEM((n, tile_rows, tile_cols), jnp.bfloat16),
            pltpu.VMEM((n, tile_rows, tile_cols), jnp.bfloat16),
            pltpu.VMEM((2, 4, tile_rows, tile_cols + 2 * BLOCK), jnp.bfloat16),
            pltpu.VMEM((2, tile_rows, tile_cols), jnp.float32),
            pltpu.VMEM((2, n, SPILL, tile_cols), jnp.bfloat16),
            pltpu.VMEM((2, n, SPILL, tile_cols), jnp.bfloat16),
            pltpu.SemaphoreType.DMA((n,)),
            pltpu.SemaphoreType.DMA((n + 1,)),
            pltpu.SemaphoreType.DMA((n,)),
            pltpu.SemaphoreType.DMA((n,)),
            pltpu.SemaphoreType.DMA((2, n)),
            pltpu.SemaphoreType.DMA((2, n)),
            pltpu.SemaphoreType.DMA((bands - 1,)),
            pltpu.SemaphoreType.DMA((bands - 1,)),
            pltpu.SemaphoreType.DMA((2, 3)),
        ],
        compiler_params=pltpu.CompilerParams(collective_id=0, has_side_effects=True),
        name="correlate_and_reduce",
    )(depth, basis, across, down)
    part = pl.BlockSpec((tile_rows // 2, tile_cols), lambda i: (i, 0))
    coadd, detection = pl.pallas_call(
        finish_kernel,
        grid=(2,),
        out_shape=(whole, whole),
        in_specs=[part] * 3
        + [pl.BlockSpec((bands - 1, tile_rows // 2, tile_cols), lambda i: (0, i, 0))],
        out_specs=(part, part),
        name="finish",
    )(numerator, denominator, det_mine, det_theirs)
    return coadd[None], detection


def solution(mesh):
    return jax.shard_map(
        functools.partial(local, dict(mesh.shape)),
        mesh=mesh,
        in_specs=(
            P(("patch", "band"), "tile", "exp", None, None),
            P(("patch", "band"), "tile", "exp", None, None),
            P(("patch", "band"), "tile", "exp"),
            P(("patch", "band"), "tile", "exp", None),
            P(("patch", "band"), "tile", "exp"),
            P(("patch", "band"), "tile", "exp"),
            P(),
        ),
        out_specs=(P(("patch", "band"), "tile", "exp"), P(("patch", "tile"), "exp")),
        check_vma=False,
    )
```

```python
import functools

import jax
import jax.numpy as jnp
import numpy as np
from jax import lax
from jax.experimental import pallas as pl
from jax.experimental.pallas import tpu as pltpu
from jax.sharding import PartitionSpec as P

BLOCK = 128
TAPS = 41
BLOCK_ROWS = 2
BLOCK_COLS = 4
SPILL = 24

kernel_sigmas = (1.0, 2.5, 6.0)
MESH = pl.DeviceIdType.MESH


def tap_matrix(rows, cols, shift):
    half_span = TAPS // 2
    offset = np.arange(rows)[:, None] - np.arange(cols)[None, :] - shift
    axis = np.arange(-half_span, half_span + 1).astype(np.float64)
    result = []
    for spread in kernel_sigmas:
        norm = np.sum(np.exp(-axis * axis / (2.0 * spread * spread)))
        result.append(
            np.where(
                np.abs(offset) <= half_span,
                np.exp(-offset * offset / (2.0 * spread * spread)),
                0.0,
            )
            / norm
        )
    return np.stack(result)


def tap_pair(taps):
    high = taps.astype(jnp.bfloat16)
    low = (taps - high.astype(np.float64)).astype(jnp.bfloat16)
    return jnp.asarray(np.stack([high, low]))


def split(value):
    high = value.astype(jnp.bfloat16)
    return high, (value - high.astype(jnp.float32)).astype(jnp.bfloat16)


def products(pairs):
    total = None
    for left, right in pairs:
        term = jnp.dot(left, right, preferred_element_type=jnp.float32)
        total = term if total is None else total + term
    return total


def place_kernel(
    held, routes, slots, kernels, inverse, coefs, images, masks, depth, basis, acc
):
    d = pl.program_id(0)
    acc[...] = jnp.zeros_like(acc)

    def one(i, carry):
        @pl.when(routes[i] == d)
        def _():
            slot = slots[i]
            which = kernels[i]
            rows = pl.ds(pl.multiple_of(slot // BLOCK_COLS * BLOCK, BLOCK), BLOCK)
            cols = pl.ds(pl.multiple_of(slot % BLOCK_COLS * BLOCK, BLOCK), BLOCK)
            bits = masks[i]
            suspect = jnp.bitwise_and(bits, 1).astype(jnp.float32)
            usable = jnp.where(jnp.bitwise_and(bits, 6) == 6, 0.0, 1.0 - 0.5 * suspect)
            scaled = usable * inverse[i]
            weighted = (
                (scaled * images[i].astype(jnp.float32)).astype(jnp.bfloat16).astype(jnp.float32)
            )
            weight = scaled.astype(jnp.bfloat16).astype(jnp.float32)
            for k in range(3):
                acc[k, rows, cols] += coefs[k, which] * weighted
            acc[3, rows, cols] += weight

        return carry

    lax.fori_loop(0, held, one, 0)
    depth[0] = acc[3].astype(jnp.bfloat16)
    basis[0, 0], basis[0, 1] = split(acc[0])
    basis[0, 2] = acc[1].astype(jnp.bfloat16)
    basis[0, 3] = acc[2].astype(jnp.bfloat16)


def reduce_kernel(
    n, strips, bands, depth, basis, across, down, numerator, denominator, det_mine, det_theirs,
    moving, outgoing, incoming, framed, result, spilling, spilled,
    send_sem, recv_sem, match_send, match_recv,
    spill_send, spill_recv, det_send, det_recv, frame_sem,
):
    me = lax.axis_index("exp")
    strip = lax.axis_index("tile")
    band = lax.axis_index("band")
    rows_all = depth.shape[1]
    chunk = 32
    barrier = pltpu.get_barrier_semaphore()
    greet = [
        (strip > 0, {"tile": strip - 1}),
        (strip < strips - 1, {"tile": strip + 1}),
    ]
    for here, peer in greet:

        @pl.when(here)
        def _(peer=peer):
            pl.semaphore_signal(barrier, inc=1, device_id=peer, device_id_type=MESH)

    for j in range(1, n):
        pl.semaphore_signal(
            barrier, inc=1, device_id={"exp": lax.rem(me + j, n)}, device_id_type=MESH
        )
    for j in range(1, bands):
        pl.semaphore_signal(
            barrier, inc=1, device_id={"band": lax.rem(band + j, bands)}, device_id_type=MESH
        )
    peers = bands - 1 + n - 1
    for here, _peer in greet:
        peers = peers + here.astype(jnp.int32)
    pl.semaphore_wait(barrier, peers)

    tile_cols = depth.shape[2]
    half = tile_cols // 2

    def frame_copies(j, slot):
        d = lax.rem(me + j, n)
        before = jnp.maximum(d - 1, 0)
        after = jnp.minimum(d + 1, n - 1)
        whole = pl.ds(BLOCK, tile_cols)
        return (
            pltpu.make_async_copy(
                basis.at[d], framed.at[slot, :, :, whole], frame_sem.at[slot, 0]
            ),
            pltpu.make_async_copy(
                basis.at[before, :, :, pl.ds(tile_cols - BLOCK, BLOCK)],
                framed.at[slot, :, :, pl.ds(0, BLOCK)],
                frame_sem.at[slot, 1],
            ),
            pltpu.make_async_copy(
                basis.at[after, :, :, pl.ds(0, BLOCK)],
                framed.at[slot, :, :, pl.ds(BLOCK + tile_cols, BLOCK)],
                frame_sem.at[slot, 2],
            ),
        )

    def spill_copy(side, j):
        peer = strip + 1 if side == 0 else strip - 1
        return pltpu.make_async_remote_copy(
            src_ref=spilling.at[side, j],
            dst_ref=spilled.at[side, j],
            send_sem=spill_send.at[side, j],
            recv_sem=spill_recv.at[side, j],
            device_id={"tile": peer},
            device_id_type=MESH,
        )

    sends_spill = (strip < strips - 1, strip > 0)
    gets_spill = (strip > 0, strip < strips - 1)
    for side in range(2):

        @pl.when(jnp.logical_not(gets_spill[side]))
        def _(side=side):
            spilled[side] = jnp.zeros(spilled.shape[1:], spilled.dtype)

    def correlate(j, slot):
        d = lax.rem(me + j, n)
        for copy in frame_copies(j, slot):
            copy.wait()

        @pl.when(d == 0)
        def _():
            framed[slot, :, :, 0:BLOCK] = jnp.zeros(
                framed.shape[1:3] + (BLOCK,), framed.dtype
            )

        @pl.when(d == n - 1)
        def _():
            framed[slot, :, :, BLOCK + tile_cols :] = jnp.zeros(
                framed.shape[1:3] + (BLOCK,), framed.dtype
            )

        first = (framed[slot, 0], framed[slot, 1])
        tall_high, tall_low = split(
            products(((down[0, 0], first[0]), (down[0, 0], first[1]), (down[1, 0], first[0])))
        )
        second = framed[slot, 2]
        tall_second = products(((down[0, 1], second), (down[1, 1], second))).astype(jnp.bfloat16)
        tall_third = products(((down[0, 2], framed[slot, 3]),)).astype(jnp.bfloat16)
        for h in range(2):
            cols = slice(h * half, h * half + half + 2 * BLOCK)
            total = products((
                (tall_high[:, cols], across[0, 0]),
                (tall_high[:, cols], across[1, 0]),
                (tall_low[:, cols], across[0, 0]),
                (tall_second[:, cols], across[0, 1]),
                (tall_second[:, cols], across[1, 1]),
                (tall_third[:, cols], across[0, 2]),
            ))
            out = slice(h * half, (h + 1) * half)
            result[slot, :, out] = total[SPILL : SPILL + rows_all]
            spilling[0, j, :, out] = total[SPILL + rows_all :].astype(jnp.bfloat16)
            spilling[1, j, :, out] = total[0:SPILL].astype(jnp.bfloat16)
        for side in range(2):

            @pl.when(sends_spill[side])
            def _(side=side):
                spill_copy(side, j).start()

    def unit_copy(d, right):
        place = d if right else jnp.where(d == me - 1, n, d)
        return pltpu.make_async_remote_copy(
            src_ref=moving.at[d],
            dst_ref=moving.at[place],
            send_sem=send_sem.at[d],
            recv_sem=recv_sem.at[place],
            device_id={"exp": me + 1 if right else me - 1},
            device_id_type=MESH,
        )

    def arrived(place):
        pltpu.make_async_remote_copy(
            src_ref=moving.at[place],
            dst_ref=moving.at[place],
            send_sem=send_sem.at[0],
            recv_sem=recv_sem.at[place],
            device_id={"band": lax.rem(band + 1, bands)},
            device_id_type=MESH,
        ).wait_recv()

    def pass_on(d, right, gets):
        @pl.when(gets)
        def _():
            arrived(d)
            for r in range(0, rows_all, chunk):
                rows = slice(r, r + chunk)
                moving[d, rows] = (
                    moving[d, rows].astype(jnp.float32) + depth[d, rows].astype(jnp.float32)
                ).astype(jnp.bfloat16)

        @pl.when(jnp.logical_not(gets))
        def _():
            for r in range(0, rows_all, chunk):
                moving[d, r : r + chunk] = depth[d, r : r + chunk]

        unit_copy(d, right).start()

    def match_copy(j):
        return pltpu.make_async_remote_copy(
            src_ref=outgoing.at[j],
            dst_ref=incoming.at[j],
            send_sem=match_send.at[j],
            recv_sem=match_recv.at[j],
            device_id={"exp": lax.rem(me + j, n)},
            device_id_type=MESH,
        )

    def complete(j, slot):
        for side in range(2):

            @pl.when(gets_spill[side])
            def _(side=side):
                spill_copy(side, j).wait_recv()

        low = rows_all - SPILL
        result[slot, 0:SPILL] += spilled[0, j].astype(jnp.float32)
        result[slot, low:] += spilled[1, j].astype(jnp.float32)
        if isinstance(j, int):
            numerator[...] = result[slot]
        else:
            for r in range(0, rows_all, chunk):
                outgoing[j, r : r + chunk] = result[slot, r : r + chunk].astype(jnp.bfloat16)

    def step_right(s, carry):
        @pl.when(n - 1 - s > me)
        def _():
            pass_on(n - 1 - s, True, me > 0)

        return carry

    def step_left(s, carry):
        @pl.when(s < me)
        def _():
            pass_on(s, False, me < n - 1)

        return carry

    right_first = 2 * me < n - 1
    left_first = jnp.logical_not(right_first)

    def pick(i):
        down_from = n - 1 - i
        right = jnp.where(down_from > me, down_from, down_from - 1)
        left = jnp.where(i < me, i, i + 1)
        d = jnp.where(right_first, right, left)
        return jnp.where(i == n - 1, 0, lax.rem(d - me + n, n))

    for copy in frame_copies(pick(0), 0):
        copy.start()

    @pl.when(me == 0)
    def _():
        lax.fori_loop(0, n - 1, step_right, 0)

    @pl.when(me == n - 1)
    def _():
        lax.fori_loop(0, n - 1, step_left, 0)

    def turn(i, carry):
        j = pick(i)
        slot = lax.rem(i, 2)

        @pl.when(i < n - 1)
        def _():
            for copy in frame_copies(pick(i + 1), 1 - slot):
                copy.start()

        correlate(j, slot)

        @pl.when(i > 0)
        def _():
            earlier = pick(i - 1)
            complete(earlier, 1 - slot)
            match_copy(earlier).start()

        @pl.when((i > 1) & right_first & (me > 0))
        def _():
            step_right(i - 2, 0)

        @pl.when((i > 1) & left_first & (me < n - 1))
        def _():
            step_left(i - 2, 0)

        return carry

    lax.fori_loop(0, n, turn, 0)
    complete(0, (n - 1) % 2)

    @pl.when(right_first)
    def _():
        @pl.when(me > 0)
        def _():
            lax.fori_loop(max(n - 2, 0), n - 1, step_right, 0)

        lax.fori_loop(0, n - 1, step_left, 0)

    @pl.when(left_first)
    def _():
        @pl.when(me < n - 1)
        def _():
            lax.fori_loop(max(n - 2, 0), n - 1, step_left, 0)

        lax.fori_loop(0, n - 1, step_right, 0)

    @pl.when(me > 0)
    def _():
        arrived(me)

    @pl.when(me == 0)
    def _():
        moving[me] = jnp.zeros(moving.shape[1:], moving.dtype)

    @pl.when(me < n - 1)
    def _():
        arrived(n)

    @pl.when(me == n - 1)
    def _():
        moving[n] = jnp.zeros(moving.shape[1:], moving.dtype)

    def gather(i, carry):
        j = i + 1
        match_copy(j).wait_recv()
        for r in range(0, rows_all, chunk):
            rows = slice(r, r + chunk)
            numerator[rows] += incoming[j, rows].astype(jnp.float32)
        return carry

    lax.fori_loop(0, n - 1, gather, 0)
    def det_copy(j, h):
        rows = pl.ds(h * rows_all // 2, rows_all // 2)
        return pltpu.make_async_remote_copy(
            src_ref=det_mine.at[rows],
            dst_ref=det_theirs.at[j - 1, rows],
            send_sem=det_send.at[j - 1, h],
            recv_sem=det_recv.at[j - 1, h],
            device_id={"band": lax.rem(band + j, bands)},
            device_id_type=MESH,
        )

    for h in range(2):
        for r in range(h * rows_all // 2, (h + 1) * rows_all // 2, chunk):
            rows = slice(r, r + chunk)
            below = 1.0 + (
                depth[me, rows].astype(jnp.float32)
                + moving[me, rows].astype(jnp.float32)
                + moving[n, rows].astype(jnp.float32)
            )
            denominator[rows] = below
            value = numerator[rows] / below
            det_mine[rows] = value * value * below
        for j in range(1, bands):
            det_copy(j, h).start()
    for h in range(2):
        for j in range(1, bands):
            det_copy(j, h).wait()

    def drain(s, carry):
        to_right = n - 1 - s
        match_copy(s + 1).wait_send()

        @pl.when(to_right > me)
        def _():
            unit_copy(to_right, True).wait_send()

        @pl.when(s < me)
        def _():
            unit_copy(s, False).wait_send()

        return carry

    lax.fori_loop(0, n - 1, drain, 0)

    def drain_spill(j, carry):
        for side in range(2):

            @pl.when(sends_spill[side])
            def _(side=side):
                spill_copy(side, j).wait_send()

        return carry

    lax.fori_loop(0, n, drain_spill, 0)


def finish_kernel(numerator, denominator, det_mine, det_theirs, coadd, detection):
    coadd[...] = numerator[...] / denominator[...]
    value = det_mine[...]
    for j in range(det_theirs.shape[0]):
        value += det_theirs[j]
    detection[...] = value


def local(sizes, images, mask_bits, inv_var, routes, block_slot, kernel_index, coefficients):
    n, strips, bands = sizes["exp"], sizes["tile"], sizes["band"]
    held = images.shape[2]
    tile_rows = BLOCK_ROWS * BLOCK
    tile_cols = BLOCK_COLS * BLOCK
    half = tile_cols // 2
    across = tap_pair(tap_matrix(2 * half, half, BLOCK))
    down = tap_pair(tap_matrix(tile_rows + 2 * SPILL, tile_rows, SPILL))
    smem = pl.BlockSpec(memory_space=pltpu.SMEM)
    vmem = pl.BlockSpec(memory_space=pltpu.VMEM)
    depth, basis = pl.pallas_call(
        functools.partial(place_kernel, held),
        grid=(n,),
        out_shape=(
            jax.ShapeDtypeStruct((n, tile_rows, tile_cols), jnp.bfloat16),
            jax.ShapeDtypeStruct((n, 4, tile_rows, tile_cols), jnp.bfloat16),
        ),
        in_specs=[smem] * 5 + [vmem] * 2,
        out_specs=(
            pl.BlockSpec((1, tile_rows, tile_cols), lambda d: (d, 0, 0)),
            pl.BlockSpec((1, 4, tile_rows, tile_cols), lambda d: (d, 0, 0, 0)),
        ),
        scratch_shapes=[pltpu.VMEM((4, tile_rows, tile_cols), jnp.float32)],
        name="place",
    )(
        routes[0, 0, :, 0], block_slot[0, 0], kernel_index[0, 0], inv_var[0, 0],
        coefficients.T, images[0, 0], mask_bits[0, 0],
    )
    whole = jax.ShapeDtypeStruct((tile_rows, tile_cols), jnp.float32)
    others = jax.ShapeDtypeStruct((bands - 1, tile_rows, tile_cols), jnp.float32)
    numerator, denominator, det_mine, det_theirs = pl.pallas_call(
        functools.partial(reduce_kernel, n, strips, bands),
        out_shape=(whole, whole, whole, others),
        in_specs=[vmem, pl.BlockSpec(memory_space=pl.ANY), vmem, vmem],
        out_specs=(vmem,) * 4,
        scratch_shapes=[
            pltpu.VMEM((n + 1, tile_rows, tile_cols), jnp.bfloat16),
            pltpu.VMEM((n, tile_rows, tile_cols), jnp.bfloat16),
            pltpu.VMEM((n, tile_rows, tile_cols), jnp.bfloat16),
            pltpu.VMEM((2, 4, tile_rows, tile_cols + 2 * BLOCK), jnp.bfloat16),
            pltpu.VMEM((2, tile_rows, tile_cols), jnp.float32),
            pltpu.VMEM((2, n, SPILL, tile_cols), jnp.bfloat16),
            pltpu.VMEM((2, n, SPILL, tile_cols), jnp.bfloat16),
            pltpu.SemaphoreType.DMA((n,)),
            pltpu.SemaphoreType.DMA((n + 1,)),
            pltpu.SemaphoreType.DMA((n,)),
            pltpu.SemaphoreType.DMA((n,)),
            pltpu.SemaphoreType.DMA((2, n)),
            pltpu.SemaphoreType.DMA((2, n)),
            pltpu.SemaphoreType.DMA((bands - 1, 2)),
            pltpu.SemaphoreType.DMA((bands - 1, 2)),
            pltpu.SemaphoreType.DMA((2, 3)),
        ],
        compiler_params=pltpu.CompilerParams(collective_id=0, has_side_effects=True),
        name="correlate_and_reduce",
    )(depth, basis, across, down)
    part = pl.BlockSpec((tile_rows // 2, tile_cols), lambda i: (i, 0))
    coadd, detection = pl.pallas_call(
        finish_kernel,
        grid=(2,),
        out_shape=(whole, whole),
        in_specs=[part] * 3
        + [pl.BlockSpec((bands - 1, tile_rows // 2, tile_cols), lambda i: (0, i, 0))],
        out_specs=(part, part),
        name="finish",
    )(numerator, denominator, det_mine, det_theirs)
    return coadd[None], detection


def solution(mesh):
    return jax.shard_map(
        functools.partial(local, dict(mesh.shape)),
        mesh=mesh,
        in_specs=(
            P(("patch", "band"), "tile", "exp", None, None),
            P(("patch", "band"), "tile", "exp", None, None),
            P(("patch", "band"), "tile", "exp"),
            P(("patch", "band"), "tile", "exp", None),
            P(("patch", "band"), "tile", "exp"),
            P(("patch", "band"), "tile", "exp"),
            P(),
        ),
        out_specs=(P(("patch", "band"), "tile", "exp"), P(("patch", "tile"), "exp")),
        check_vma=False,
    )
```

```python
import functools

import jax
import jax.numpy as jnp
import numpy as np
from jax import lax
from jax.experimental import pallas as pl
from jax.experimental.pallas import tpu as pltpu
from jax.sharding import PartitionSpec as P

BLOCK = 128
TAPS = 41
BLOCK_ROWS = 2
BLOCK_COLS = 4
SPILL = 24

kernel_sigmas = (1.0, 2.5, 6.0)
MESH = pl.DeviceIdType.MESH


def tap_matrix(rows, cols, shift):
    half_span = TAPS // 2
    offset = np.arange(rows)[:, None] - np.arange(cols)[None, :] - shift
    axis = np.arange(-half_span, half_span + 1).astype(np.float64)
    result = []
    for spread in kernel_sigmas:
        norm = np.sum(np.exp(-axis * axis / (2.0 * spread * spread)))
        result.append(
            np.where(
                np.abs(offset) <= half_span,
                np.exp(-offset * offset / (2.0 * spread * spread)),
                0.0,
            )
            / norm
        )
    return np.stack(result)


def tap_pair(taps):
    high = taps.astype(jnp.bfloat16)
    low = (taps - high.astype(np.float64)).astype(jnp.bfloat16)
    return jnp.asarray(np.stack([high, low]))


def split(value):
    high = value.astype(jnp.bfloat16)
    return high, (value - high.astype(jnp.float32)).astype(jnp.bfloat16)


def products(pairs):
    total = None
    for left, right in pairs:
        term = jnp.dot(left, right, preferred_element_type=jnp.float32)
        total = term if total is None else total + term
    return total


def place_kernel(
    held, routes, slots, kernels, inverse, coefs, images, masks, depth, basis, acc
):
    d = pl.program_id(0)
    acc[...] = jnp.zeros_like(acc)

    def one(i, carry):
        @pl.when(routes[i] == d)
        def _():
            slot = slots[i]
            which = kernels[i]
            rows = pl.ds(pl.multiple_of(slot // BLOCK_COLS * BLOCK, BLOCK), BLOCK)
            cols = pl.ds(pl.multiple_of(slot % BLOCK_COLS * BLOCK, BLOCK), BLOCK)
            bits = masks[i]
            suspect = jnp.bitwise_and(bits, 1).astype(jnp.float32)
            usable = jnp.where(jnp.bitwise_and(bits, 6) == 6, 0.0, 1.0 - 0.5 * suspect)
            scaled = usable * inverse[i]
            weighted = (
                (scaled * images[i].astype(jnp.float32)).astype(jnp.bfloat16).astype(jnp.float32)
            )
            weight = scaled.astype(jnp.bfloat16).astype(jnp.float32)
            for k in range(3):
                acc[k, rows, cols] += coefs[k, which] * weighted
            acc[3, rows, cols] += weight

        return carry

    lax.fori_loop(0, held, one, 0)
    depth[0] = acc[3].astype(jnp.bfloat16)
    basis[0, 0], basis[0, 1] = split(acc[0])
    basis[0, 2] = acc[1].astype(jnp.bfloat16)
    basis[0, 3] = acc[2].astype(jnp.bfloat16)


def reduce_kernel(
    n, strips, bands, depth, basis, across, down, numerator, denominator, det_mine, det_theirs,
    moving, outgoing, incoming, framed, result, spilling, spilled,
    send_sem, recv_sem, match_send, match_recv,
    spill_send, spill_recv, det_send, det_recv, frame_sem,
):
    me = lax.axis_index("exp")
    strip = lax.axis_index("tile")
    band = lax.axis_index("band")
    rows_all = depth.shape[1]
    chunk = 32
    barrier = pltpu.get_barrier_semaphore()
    greet = [
        (strip > 0, {"tile": strip - 1}),
        (strip < strips - 1, {"tile": strip + 1}),
    ]
    for here, peer in greet:

        @pl.when(here)
        def _(peer=peer):
            pl.semaphore_signal(barrier, inc=1, device_id=peer, device_id_type=MESH)

    for j in range(1, n):
        pl.semaphore_signal(
            barrier, inc=1, device_id={"exp": lax.rem(me + j, n)}, device_id_type=MESH
        )
    for j in range(1, bands):
        pl.semaphore_signal(
            barrier, inc=1, device_id={"band": lax.rem(band + j, bands)}, device_id_type=MESH
        )
    peers = bands - 1 + n - 1
    for here, _peer in greet:
        peers = peers + here.astype(jnp.int32)
    pl.semaphore_wait(barrier, peers)

    tile_cols = depth.shape[2]
    half = tile_cols // 2

    def frame_copies(j, slot):
        d = lax.rem(me + j, n)
        before = jnp.maximum(d - 1, 0)
        after = jnp.minimum(d + 1, n - 1)
        whole = pl.ds(BLOCK, tile_cols)
        return (
            pltpu.make_async_copy(
                basis.at[d], framed.at[slot, :, :, whole], frame_sem.at[slot, 0]
            ),
            pltpu.make_async_copy(
                basis.at[before, :, :, pl.ds(tile_cols - BLOCK, BLOCK)],
                framed.at[slot, :, :, pl.ds(0, BLOCK)],
                frame_sem.at[slot, 1],
            ),
            pltpu.make_async_copy(
                basis.at[after, :, :, pl.ds(0, BLOCK)],
                framed.at[slot, :, :, pl.ds(BLOCK + tile_cols, BLOCK)],
                frame_sem.at[slot, 2],
            ),
        )

    def spill_copy(side, j):
        peer = strip + 1 if side == 0 else strip - 1
        return pltpu.make_async_remote_copy(
            src_ref=spilling.at[side, j],
            dst_ref=spilled.at[side, j],
            send_sem=spill_send.at[side, j],
            recv_sem=spill_recv.at[side, j],
            device_id={"tile": peer},
            device_id_type=MESH,
        )

    sends_spill = (strip < strips - 1, strip > 0)
    gets_spill = (strip > 0, strip < strips - 1)
    for side in range(2):

        @pl.when(jnp.logical_not(gets_spill[side]))
        def _(side=side):
            spilled[side] = jnp.zeros(spilled.shape[1:], spilled.dtype)

    def correlate(j, slot):
        d = lax.rem(me + j, n)
        for copy in frame_copies(j, slot):
            copy.wait()

        @pl.when(d == 0)
        def _():
            framed[slot, :, :, 0:BLOCK] = jnp.zeros(
                framed.shape[1:3] + (BLOCK,), framed.dtype
            )

        @pl.when(d == n - 1)
        def _():
            framed[slot, :, :, BLOCK + tile_cols :] = jnp.zeros(
                framed.shape[1:3] + (BLOCK,), framed.dtype
            )

        first = (framed[slot, 0], framed[slot, 1])
        tall_high, tall_low = split(
            products(((down[0, 0], first[0]), (down[0, 0], first[1]), (down[1, 0], first[0])))
        )
        second = framed[slot, 2]
        tall_second = products(((down[0, 1], second), (down[1, 1], second))).astype(jnp.bfloat16)
        tall_third = products(((down[0, 2], framed[slot, 3]),)).astype(jnp.bfloat16)
        for h in range(2):
            cols = slice(h * half, h * half + half + 2 * BLOCK)
            total = products((
                (tall_high[:, cols], across[0, 0]),
                (tall_high[:, cols], across[1, 0]),
                (tall_low[:, cols], across[0, 0]),
                (tall_second[:, cols], across[0, 1]),
                (tall_second[:, cols], across[1, 1]),
                (tall_third[:, cols], across[0, 2]),
            ))
            out = slice(h * half, (h + 1) * half)
            result[slot, :, out] = total[SPILL : SPILL + rows_all]
            spilling[0, j, :, out] = total[SPILL + rows_all :].astype(jnp.bfloat16)
            spilling[1, j, :, out] = total[0:SPILL].astype(jnp.bfloat16)
        for side in range(2):

            @pl.when(sends_spill[side])
            def _(side=side):
                spill_copy(side, j).start()

    def unit_copy(d, right):
        place = d if right else jnp.where(d == me - 1, n, d)
        return pltpu.make_async_remote_copy(
            src_ref=moving.at[d],
            dst_ref=moving.at[place],
            send_sem=send_sem.at[d],
            recv_sem=recv_sem.at[place],
            device_id={"exp": me + 1 if right else me - 1},
            device_id_type=MESH,
        )

    def arrived(place):
        pltpu.make_async_remote_copy(
            src_ref=moving.at[place],
            dst_ref=moving.at[place],
            send_sem=send_sem.at[0],
            recv_sem=recv_sem.at[place],
            device_id={"band": lax.rem(band + 1, bands)},
            device_id_type=MESH,
        ).wait_recv()

    def pass_on(d, right, gets):
        @pl.when(gets)
        def _():
            arrived(d)
            for r in range(0, rows_all, chunk):
                rows = slice(r, r + chunk)
                moving[d, rows] = (
                    moving[d, rows].astype(jnp.float32) + depth[d, rows].astype(jnp.float32)
                ).astype(jnp.bfloat16)

        @pl.when(jnp.logical_not(gets))
        def _():
            for r in range(0, rows_all, chunk):
                moving[d, r : r + chunk] = depth[d, r : r + chunk]

        unit_copy(d, right).start()

    def match_copy(j):
        return pltpu.make_async_remote_copy(
            src_ref=outgoing.at[j],
            dst_ref=incoming.at[j],
            send_sem=match_send.at[j],
            recv_sem=match_recv.at[j],
            device_id={"exp": lax.rem(me + j, n)},
            device_id_type=MESH,
        )

    def complete(j, slot):
        for side in range(2):

            @pl.when(gets_spill[side])
            def _(side=side):
                spill_copy(side, j).wait_recv()

        low = rows_all - SPILL
        result[slot, 0:SPILL] += spilled[0, j].astype(jnp.float32)
        result[slot, low:] += spilled[1, j].astype(jnp.float32)
        if isinstance(j, int):
            numerator[...] = result[slot]
        else:
            for r in range(0, rows_all, chunk):
                outgoing[j, r : r + chunk] = result[slot, r : r + chunk].astype(jnp.bfloat16)

    def step_right(s, carry):
        @pl.when(n - 1 - s > me)
        def _():
            pass_on(n - 1 - s, True, me > 0)

        return carry

    def step_left(s, carry):
        @pl.when(s < me)
        def _():
            pass_on(s, False, me < n - 1)

        return carry

    right_first = 2 * me < n - 1
    left_first = jnp.logical_not(right_first)

    def pick(i):
        down_from = n - 1 - i
        right = jnp.where(down_from > me, down_from, down_from - 1)
        left = jnp.where(i < me, i, i + 1)
        d = jnp.where(right_first, right, left)
        return jnp.where(i == n - 1, 0, lax.rem(d - me + n, n))

    for copy in frame_copies(pick(0), 0):
        copy.start()

    @pl.when(me == 0)
    def _():
        lax.fori_loop(0, n - 1, step_right, 0)

    @pl.when(me == n - 1)
    def _():
        lax.fori_loop(0, n - 1, step_left, 0)

    def turn(i, carry):
        j = pick(i)
        slot = lax.rem(i, 2)

        @pl.when(i < n - 1)
        def _():
            for copy in frame_copies(pick(i + 1), 1 - slot):
                copy.start()

        correlate(j, slot)

        @pl.when(i > 0)
        def _():
            earlier = pick(i - 1)
            complete(earlier, 1 - slot)
            match_copy(earlier).start()

        @pl.when((i > 0) & right_first & (me > 0))
        def _():
            step_right(i - 1, 0)

        @pl.when((i > 0) & left_first & (me < n - 1))
        def _():
            step_left(i - 1, 0)

        return carry

    lax.fori_loop(0, n, turn, 0)
    complete(0, (n - 1) % 2)

    @pl.when(right_first)
    def _():
        @pl.when(me > 0)
        def _():
            lax.fori_loop(n - 1, n - 1, step_right, 0)

        lax.fori_loop(0, n - 1, step_left, 0)

    @pl.when(left_first)
    def _():
        @pl.when(me < n - 1)
        def _():
            lax.fori_loop(n - 1, n - 1, step_left, 0)

        lax.fori_loop(0, n - 1, step_right, 0)

    @pl.when(me > 0)
    def _():
        arrived(me)

    @pl.when(me == 0)
    def _():
        moving[me] = jnp.zeros(moving.shape[1:], moving.dtype)

    @pl.when(me < n - 1)
    def _():
        arrived(n)

    @pl.when(me == n - 1)
    def _():
        moving[n] = jnp.zeros(moving.shape[1:], moving.dtype)

    def gather(i, carry):
        j = i + 1
        match_copy(j).wait_recv()
        for r in range(0, rows_all, chunk):
            rows = slice(r, r + chunk)
            numerator[rows] += incoming[j, rows].astype(jnp.float32)
        return carry

    lax.fori_loop(0, n - 1, gather, 0)
    def det_copy(j, h):
        rows = pl.ds(h * rows_all // 2, rows_all // 2)
        return pltpu.make_async_remote_copy(
            src_ref=det_mine.at[rows],
            dst_ref=det_theirs.at[j - 1, rows],
            send_sem=det_send.at[j - 1, h],
            recv_sem=det_recv.at[j - 1, h],
            device_id={"band": lax.rem(band + j, bands)},
            device_id_type=MESH,
        )

    for h in range(2):
        for r in range(h * rows_all // 2, (h + 1) * rows_all // 2, chunk):
            rows = slice(r, r + chunk)
            below = 1.0 + (
                depth[me, rows].astype(jnp.float32)
                + moving[me, rows].astype(jnp.float32)
                + moving[n, rows].astype(jnp.float32)
            )
            denominator[rows] = below
            value = numerator[rows] / below
            det_mine[rows] = value * value * below
        for j in range(1, bands):
            det_copy(j, h).start()
    for h in range(2):
        for j in range(1, bands):
            det_copy(j, h).wait()

    def drain(s, carry):
        to_right = n - 1 - s
        match_copy(s + 1).wait_send()

        @pl.when(to_right > me)
        def _():
            unit_copy(to_right, True).wait_send()

        @pl.when(s < me)
        def _():
            unit_copy(s, False).wait_send()

        return carry

    lax.fori_loop(0, n - 1, drain, 0)

    def drain_spill(j, carry):
        for side in range(2):

            @pl.when(sends_spill[side])
            def _(side=side):
                spill_copy(side, j).wait_send()

        return carry

    lax.fori_loop(0, n, drain_spill, 0)


def finish_kernel(numerator, denominator, det_mine, det_theirs, coadd, detection):
    coadd[...] = numerator[...] / denominator[...]
    value = det_mine[...]
    for j in range(det_theirs.shape[0]):
        value += det_theirs[j]
    detection[...] = value


def local(sizes, images, mask_bits, inv_var, routes, block_slot, kernel_index, coefficients):
    n, strips, bands = sizes["exp"], sizes["tile"], sizes["band"]
    held = images.shape[2]
    tile_rows = BLOCK_ROWS * BLOCK
    tile_cols = BLOCK_COLS * BLOCK
    half = tile_cols // 2
    across = tap_pair(tap_matrix(2 * half, half, BLOCK))
    down = tap_pair(tap_matrix(tile_rows + 2 * SPILL, tile_rows, SPILL))
    smem = pl.BlockSpec(memory_space=pltpu.SMEM)
    vmem = pl.BlockSpec(memory_space=pltpu.VMEM)
    depth, basis = pl.pallas_call(
        functools.partial(place_kernel, held),
        grid=(n,),
        out_shape=(
            jax.ShapeDtypeStruct((n, tile_rows, tile_cols), jnp.bfloat16),
            jax.ShapeDtypeStruct((n, 4, tile_rows, tile_cols), jnp.bfloat16),
        ),
        in_specs=[smem] * 5 + [vmem] * 2,
        out_specs=(
            pl.BlockSpec((1, tile_rows, tile_cols), lambda d: (d, 0, 0)),
            pl.BlockSpec((1, 4, tile_rows, tile_cols), lambda d: (d, 0, 0, 0)),
        ),
        scratch_shapes=[pltpu.VMEM((4, tile_rows, tile_cols), jnp.float32)],
        name="place",
    )(
        routes[0, 0, :, 0], block_slot[0, 0], kernel_index[0, 0], inv_var[0, 0],
        coefficients.T, images[0, 0], mask_bits[0, 0],
    )
    whole = jax.ShapeDtypeStruct((tile_rows, tile_cols), jnp.float32)
    others = jax.ShapeDtypeStruct((bands - 1, tile_rows, tile_cols), jnp.float32)
    numerator, denominator, det_mine, det_theirs = pl.pallas_call(
        functools.partial(reduce_kernel, n, strips, bands),
        out_shape=(whole, whole, whole, others),
        in_specs=[vmem, pl.BlockSpec(memory_space=pl.ANY), vmem, vmem],
        out_specs=(vmem,) * 4,
        scratch_shapes=[
            pltpu.VMEM((n + 1, tile_rows, tile_cols), jnp.bfloat16),
            pltpu.VMEM((n, tile_rows, tile_cols), jnp.bfloat16),
            pltpu.VMEM((n, tile_rows, tile_cols), jnp.bfloat16),
            pltpu.VMEM((2, 4, tile_rows, tile_cols + 2 * BLOCK), jnp.bfloat16),
            pltpu.VMEM((2, tile_rows, tile_cols), jnp.float32),
            pltpu.VMEM((2, n, SPILL, tile_cols), jnp.bfloat16),
            pltpu.VMEM((2, n, SPILL, tile_cols), jnp.bfloat16),
            pltpu.SemaphoreType.DMA((n,)),
            pltpu.SemaphoreType.DMA((n + 1,)),
            pltpu.SemaphoreType.DMA((n,)),
            pltpu.SemaphoreType.DMA((n,)),
            pltpu.SemaphoreType.DMA((2, n)),
            pltpu.SemaphoreType.DMA((2, n)),
            pltpu.SemaphoreType.DMA((bands - 1, 2)),
            pltpu.SemaphoreType.DMA((bands - 1, 2)),
            pltpu.SemaphoreType.DMA((2, 3)),
        ],
        compiler_params=pltpu.CompilerParams(collective_id=0, has_side_effects=True),
        name="correlate_and_reduce",
    )(depth, basis, across, down)
    part = pl.BlockSpec((tile_rows // 4, tile_cols), lambda i: (i, 0))
    coadd, detection = pl.pallas_call(
        finish_kernel,
        grid=(4,),
        out_shape=(whole, whole),
        in_specs=[part] * 3
        + [pl.BlockSpec((bands - 1, tile_rows // 4, tile_cols), lambda i: (0, i, 0))],
        out_specs=(part, part),
        name="finish",
    )(numerator, denominator, det_mine, det_theirs)
    return coadd[None], detection


def solution(mesh):
    return jax.shard_map(
        functools.partial(local, dict(mesh.shape)),
        mesh=mesh,
        in_specs=(
            P(("patch", "band"), "tile", "exp", None, None),
            P(("patch", "band"), "tile", "exp", None, None),
            P(("patch", "band"), "tile", "exp"),
            P(("patch", "band"), "tile", "exp", None),
            P(("patch", "band"), "tile", "exp"),
            P(("patch", "band"), "tile", "exp"),
            P(),
        ),
        out_specs=(P(("patch", "band"), "tile", "exp"), P(("patch", "tile"), "exp")),
        check_vma=False,
    )
```
